32 devices in a mesh: energy: 8 (over y, x, core), elem: 4 (over z).
Axes of the slice: x: 2, y: 2, z: 4, core: 2. Of those that a mesh axis runs over, the one named last changes fastest.
Arguments:
- g_lesser: bfloat16 [2, 512, 2048], P(None, 'energy', 'elem'), may hold values from -6 to 6
- g_greater: bfloat16 [2, 512, 2048], P(None, 'energy', 'elem'), may hold values from -6 to 6
- send_rows: int32 [4, 8, 4, 32], P('elem'), may hold values from 0 to 63, as said below
- partner_slot: int32 [2048], P('elem'), may hold values from 0 to 127, as said below
Outputs:
- polarization_lesser: bfloat16 [2, 512, 2048], P(None, 'energy', 'elem')
- polarization_greater: bfloat16 [2, 512, 2048], P(None, 'energy', 'elem')
The draws below stay inside these ranges and needn't reach their ends.
Inputs may be any that keep to these rules, and one draw needn't show every extreme that they name: partner is an involution on the elements that keeps the element piece n. The groups fall into two halves of 2 groups; for a sending group b and element piece n, send_rows[b, n, a, :] lists 32 distinct rows when a lies in b's half (b itself included) and zeros otherwise; every row of that piece of the sender appears exactly once over all receivers of its half. `partner_slot`: every slot named points into a receiving group's half and to a slot that carries a row; the 64 elements of one element piece of a group name 64 distinct slots.
All inputs are finite; a program needn't handle non-finite values.
Results may differ from the reference program's by a relative error of at most 0.001.
Values may be sent and summed in bfloat16 or wider, within the bound.
No kernel may reach another device: no remote copies, remote signals or barrier semaphores. Data moves between devices by JAX's collectives and lax.ppermute only.
A program may use at most 64 MiB of HBM per device.

```python
import jax
import jax.numpy as jnp
from jax import lax

ELEM_DEV = 64
NE = 512
GROUPS = 4
PIECES = 8
GROUP = 512
ELEMS = 2048
CAP = 32


def pair_lists(key):
    base_key = jax.random.fold_in(key, 4711)
    piece_keys = jax.random.split(base_key, PIECES)
    half_count = GROUPS // 2

    def one_piece(piece_key):
        order_key, rows_key = jax.random.split(piece_key)
        group_order = jax.random.permutation(order_key, GROUPS).astype(jnp.int32)
        rank_of = jnp.argsort(group_order, stable=True).astype(jnp.int32)
        group_class = rank_of // half_count
        class_index = rank_of % half_count
        row_keys = jax.random.split(rows_key, GROUPS)
        row_order = jax.vmap(lambda row_key: jax.random.permutation(row_key, ELEM_DEV).astype(jnp.int32))(row_keys)
        slot_range = jnp.arange(CAP, dtype=jnp.int32)
        positions = (class_index[:, None] * CAP + slot_range[None, :]).reshape(-1)
        gathered = jnp.take(row_order, positions, axis=1).reshape(GROUPS, GROUPS, CAP)
        same_half = group_class[:, None] == group_class[None, :]
        send_table = jnp.where(same_half[:, :, None], gathered, jnp.zeros_like(gathered)).astype(jnp.int32)
        place_of = jnp.argsort(row_order, axis=1, stable=True).astype(jnp.int32)
        segment = place_of // CAP
        within = place_of % CAP
        peer_group = jnp.take(group_order, group_class[:, None] * half_count + segment)
        own_group = jnp.arange(GROUPS, dtype=jnp.int32)[:, None]
        partner_within = jnp.where(peer_group == own_group, jnp.bitwise_xor(within, 1), within)
        slot_table = (peer_group * CAP + partner_within).astype(jnp.int32)
        return (send_table, slot_table)
    send_all, slot_all = jax.vmap(one_piece)(piece_keys)
    return (send_all, slot_all)


def draw_send_rows(key, part):
    send_all, slot_all = pair_lists(key)
    return jnp.transpose(send_all, (1, 0, 2, 3)).astype(jnp.int32)


def draw_partner_slot(key, part):
    send_all, slot_all = pair_lists(key)
    return jnp.transpose(slot_all, (1, 0, 2)).reshape(ELEMS).astype(jnp.int32)


def levels(rng, extent, cuts, smallest, high):
    def one(dim, parts):
        draws = jax.random.uniform(jax.random.fold_in(jax.random.fold_in(rng, 6), dim), (parts,), jnp.float32, smallest / len(cuts), high / len(cuts))
        return jnp.repeat(jnp.exp(draws), extent[dim] // parts).reshape((-1,) + (1,) * (len(extent) - dim - 1))

    loudness = one(*cuts[0])
    for cut in cuts[1:]:
        loudness = loudness * one(*cut)
    return loudness


def scatter_about(own_key, dims, spread, bound, cuts=(), held_as=jnp.bfloat16):
    drawn = jax.random.normal(own_key, dims, jnp.float32) * spread
    if len(cuts) > 0:
        drawn = levels(own_key, dims, cuts, -0.22, 0.18) * drawn
    return jnp.clip(drawn, min=-bound, max=bound).astype(held_as)


def setup_inputs(seed: int = 0) -> dict:
    key_list = jax.random.split(jax.random.key(seed), 5)
    g_lesser = scatter_about(key_list[0], (2, NE, ELEMS), 1.0, 6.0, ((1, 8), (2, 4)))
    g_greater = scatter_about(key_list[1], (2, NE, ELEMS), 1.0, 6.0, ((1, 8), (2, 4)))
    send_rows = draw_send_rows(jax.random.fold_in(key_list[4], 71), 0)
    partner_slot = draw_partner_slot(jax.random.fold_in(key_list[4], 71), 0)
    return {"g_lesser": g_lesser, "g_greater": g_greater, "send_rows": send_rows, "partner_slot": partner_slot}


def reverse_energy(values):
    return jnp.roll(jnp.flip(values, axis=0), 1, axis=0)

def reference(g_lesser, g_greater, send_rows, partner_slot):
    element = jnp.arange(ELEMS, dtype=jnp.int32)
    group_of = element // GROUP
    piece_of = element % GROUP // ELEM_DEV
    source_group = partner_slot // CAP
    source_slot = partner_slot % CAP
    partner_row = send_rows[source_group, piece_of, group_of, source_slot]
    partner = (source_group * GROUP + piece_of * ELEM_DEV + partner_row).astype(jnp.int32)
    scale = 1.0 / jnp.sqrt(jnp.float32(NE))

    def as_complex(table, columns):
        picked = jnp.take(table, columns, axis=2).astype(jnp.float32)
        return lax.complex(picked[0], picked[1])

    def one_group(group_index):
        columns = (group_index * GROUP + jnp.arange(GROUP, dtype=jnp.int32)).astype(jnp.int32)
        partner_columns = jnp.take(partner, columns)
        own_lesser = jnp.fft.fft(as_complex(g_lesser, columns), axis=0)
        own_greater = jnp.fft.fft(as_complex(g_greater, columns), axis=0)
        far_lesser = reverse_energy(jnp.fft.fft(as_complex(g_lesser, partner_columns), axis=0))
        far_greater = reverse_energy(jnp.fft.fft(as_complex(g_greater, partner_columns), axis=0))
        lesser_corr = jnp.fft.ifft(own_lesser * far_greater, axis=0) * -1j * scale
        greater_corr = jnp.fft.ifft(own_greater * far_lesser, axis=0) * -1j * scale
        lesser_out = jnp.stack([jnp.real(lesser_corr), jnp.imag(lesser_corr)]).astype(jnp.bfloat16)
        greater_out = jnp.stack([jnp.real(greater_corr), jnp.imag(greater_corr)]).astype(jnp.bfloat16)
        return (lesser_out, greater_out)
    lesser_all, greater_all = lax.map(one_group, jnp.arange(GROUPS, dtype=jnp.int32))
    lesser_all = jnp.moveaxis(lesser_all, 0, 2).reshape(2, NE, ELEMS)
    greater_all = jnp.moveaxis(greater_all, 0, 2).reshape(2, NE, ELEMS)
    return (lesser_all, greater_all)
```

```python
import functools
import math

import jax
import jax.numpy as jnp
import numpy as np
from jax import lax
from jax.experimental import pallas as pl
from jax.experimental.pallas import tpu as pltpu
from jax.sharding import PartitionSpec as P

BF16 = jnp.bfloat16
F32 = jnp.float32
VMEM_BYTES = 24 * 1024 * 1024


def fourier_tables(length):
    half = length // 2
    steps = np.arange(half)[:, None] * np.arange(length)[None, :] % length
    angle = steps * (2.0 * math.pi / length)
    sines = np.sin(angle)
    sines[0] = 1.0 - 2.0 * (np.arange(length) % 2)
    table = np.concatenate([np.cos(angle), sines], 0)

    def split(values):
        high = values.astype(np.float32).astype(jnp.bfloat16)
        low = (values - high.astype(np.float64)).astype(np.float32).astype(jnp.bfloat16)
        return np.stack([high, low])

    return split(table), split(table.T)


def pack_kernel(lesser_ref, greater_ref, out_ref):
    pieces, _, _, lanes = out_ref.shape
    width = lanes // 2
    for n in range(pieces):
        cols = slice(n * width, (n + 1) * width)
        out_ref[n] = jnp.concatenate([lesser_ref[:, :, cols], greater_ref[:, :, cols]], axis=-1)


def unpack_kernel(in_ref, lesser_ref, greater_ref):
    pieces, _, _, lanes = in_ref.shape
    width = lanes // 2
    per_tile = max(1, 128 // width)
    for first in range(0, pieces, per_tile):
        group = range(first, min(first + per_tile, pieces))
        cols = slice(first * width, (group[-1] + 1) * width)
        lesser_ref[:, :, cols] = jnp.concatenate([in_ref[n][:, :, :width] for n in group], axis=-1)
        greater_ref[:, :, cols] = jnp.concatenate([in_ref[n][:, :, width:] for n in group], axis=-1)


def one_hot(index_row, depth):
    rows = lax.broadcasted_iota(jnp.int32, (depth, index_row.shape[-1]), 0)
    return jnp.where(rows == index_row, 1.0, 0.0).astype(BF16)


def dot(a, b):
    return lax.dot_general(a, b, (((1,), (0,)), ((), ())), preferred_element_type=F32)


def rows_of(ref, part):
    blocks, _, energies, lanes = ref.shape
    return ref[:, part].reshape(blocks * energies, lanes)


def select_kernel(index_ref, own_ref, out_ref):
    lanes = own_ref.shape[-1]
    for part in range(2):
        picked = dot(rows_of(own_ref, part), one_hot(index_ref[part : part + 1, :], lanes))
        if part == 0:
            total = picked
        else:
            total = total + picked
    out_ref[...] = total.astype(BF16)


def correlate_kernel(index_ref, own_ref, far_ref, forward_ref, inverse_ref, out_ref):
    blocks, _, energies, lanes = own_ref.shape
    length = blocks * energies
    half = length // 2
    far = far_ref[...]
    pick_own = one_hot(index_ref[0:1, :], lanes)
    columns = [rows_of(own_ref, 0), rows_of(own_ref, 1)]
    for part in range(2):
        pick_far = one_hot(index_ref[1 + part : 2 + part, :], far.shape[-1])
        columns.append((dot(columns[part], pick_own) + dot(far, pick_far)).astype(BF16))
    signals = jnp.concatenate(columns, axis=-1)
    spectra = dot(forward_ref[0], signals) + dot(forward_ref[1], signals)
    even, odd = spectra[:half], spectra[half:]

    def split(values):
        return [values[:, i * lanes : (i + 1) * lanes] for i in range(4)]

    def combine(even, odd, odd_even):
        a_re, a_im, c_re, c_im = split(even)
        b_re, b_im, d_re, d_im = split(odd)
        u_re = a_re * c_re - a_im * c_im + (b_re * d_re - b_im * d_im)
        u_im = a_re * c_im + a_im * c_re + (b_re * d_im + b_im * d_re)
        v_re = b_re * c_re - b_im * c_im - (a_re * d_re - a_im * d_im)
        v_im = b_re * c_im + b_im * c_re - (a_re * d_im + a_im * d_re)
        return u_re, u_im, v_re, v_im

    def ends(even, odd):
        a_re, a_im, c_re, c_im = split(even)
        b_re, b_im, d_re, d_im = split(odd)
        return (
            0.5 * (a_re * c_re - a_im * c_im),
            0.5 * (a_re * c_im + a_im * c_re),
            0.5 * (b_re * d_re - b_im * d_im),
            0.5 * (b_re * d_im + b_im * d_re),
        )

    first = lax.broadcasted_iota(jnp.int32, (half, lanes), 0) == 0
    u_re, u_im, v_re, v_im = [
        jnp.where(first, end, mid) for mid, end in zip(combine(even, odd, None), ends(even, odd))
    ]
    top = jnp.concatenate([u_im, -u_re], axis=-1)
    bottom = jnp.concatenate([v_im, -v_re], axis=-1)
    products = jnp.concatenate([top, bottom], axis=0)
    high = products.astype(BF16)
    low = (products - high.astype(F32)).astype(BF16)
    back = dot(inverse_ref[0], high) + (dot(inverse_ref[0], low) + dot(inverse_ref[1], high))
    result = (back * (2.0 / (length * math.sqrt(length)))).astype(BF16)
    for part in range(2):
        out_ref[:, part] = result[:, part * lanes : (part + 1) * lanes].reshape(blocks, energies, lanes)


def call(kernel, out_shape, flops, *args):
    outs = out_shape if isinstance(out_shape, (list, tuple)) else [out_shape]
    moved = sum(math.prod(v.shape) * v.dtype.itemsize for v in [*args, *outs])
    return pl.pallas_call(
        kernel,
        out_shape=out_shape,
        compiler_params=pltpu.CompilerParams(vmem_limit_bytes=VMEM_BYTES),
        cost_estimate=pl.CostEstimate(flops=flops, bytes_accessed=moved, transcendentals=0),
    )(*args)


def shards(g_lesser, g_greater, send_rows, partner_slot):
    piece = lax.axis_index("energy")
    group = lax.axis_index("elem")
    pieces = lax.axis_size("energy")
    groups = lax.axis_size("elem")
    _, energies, group_rows = g_lesser.shape
    width = group_rows // pieces
    cap = send_rows.shape[-1]
    lanes = 2 * width
    length = pieces * energies

    packed = call(
        pack_kernel, jax.ShapeDtypeStruct((pieces, 2, energies, lanes), BF16), 0, g_lesser, g_greater
    )
    own = lax.all_to_all(packed, "energy", split_axis=0, concat_axis=0, tiled=True)

    lists = lax.dynamic_index_in_dim(send_rows[0], piece, 0, keepdims=False)
    slots = lax.dynamic_slice_in_dim(partner_slot, piece * width, width, 0)
    source, place = slots // cap, slots % cap
    if groups == 4 and cap >= 2:
        ids = jnp.arange(groups, dtype=jnp.int32)
        others = jnp.where((ids != group)[:, None], lists, 0)
        cross_rows = jnp.sum(others, axis=0)
        flip = jnp.sum(jnp.where(jnp.sum(others, axis=1) > 0, ids ^ group, 0))
        near_rows = jnp.sum(jnp.where((ids == group)[:, None], lists, 0), axis=0)
        none = jnp.full((2 * cap,), -1, jnp.int32)
        both = jnp.concatenate([cross_rows, cross_rows + width])
        picks = jnp.stack([jnp.concatenate([both, none]), jnp.concatenate([none, both])])
        outgoing = call(
            select_kernel, jax.ShapeDtypeStruct((length, 4 * cap), BF16), 4 * length * lanes * 4 * cap, picks, own
        )

        def swap(values, bit):
            return lax.ppermute(values, "elem", [(i, i ^ bit) for i in range(groups)])

        one = swap(outgoing, 1)
        two = swap(jnp.where(flip == 3, one, outgoing), 2)
        far = jnp.where(flip == 1, one, two)
        steps = jnp.arange(cap, dtype=jnp.int32)
        row = jnp.sum(jnp.where(place[:, None] == steps[None, :], near_rows[None, :], 0), axis=1)
        near = source == group
        own_row = jnp.where(near, row, -1)
        own_greater = jnp.where(near, row + width, -1)
        far_lesser = jnp.where(near, -1, place)
        far_greater = jnp.where(near, -1, place + cap)
        far_step = 2 * cap
    else:
        rows = lists.reshape(-1)
        pick = (jnp.arange(width, dtype=jnp.int32)[:, None] == rows[None, :]).astype(BF16)
        split = own.reshape(pieces, 2, energies, 2, width)
        outgoing = jnp.einsum("pceds,sm->mpced", split, pick, preferred_element_type=F32).astype(BF16)
        incoming = lax.all_to_all(outgoing, "elem", split_axis=0, concat_axis=0, tiled=True)
        far = jnp.transpose(incoming, (1, 3, 2, 4, 0)).reshape(length, 4 * groups * cap)
        own_row = jnp.full((width,), -1, jnp.int32)
        own_greater = own_row
        far_lesser = slots
        far_greater = slots + groups * cap
        far_step = 2 * groups * cap
    far_row = jnp.concatenate([far_greater, far_lesser])
    index = jnp.stack(
        [jnp.concatenate([own_greater, own_row]), far_row, jnp.where(far_row < 0, -1, far_row + far_step)]
    )
    forward, inverse = fourier_tables(length)
    result = call(
        correlate_kernel,
        jax.ShapeDtypeStruct((pieces, 2, energies, lanes), BF16),
        2 * length * length * lanes * 14,
        index,
        own,
        far,
        jnp.asarray(forward),
        jnp.asarray(inverse),
    )
    back = lax.all_to_all(result, "energy", split_axis=0, concat_axis=0, tiled=True)
    out = jax.ShapeDtypeStruct((2, energies, group_rows), BF16)
    lesser_out, greater_out = call(unpack_kernel, [out, out], 0, back)
    return (lesser_out, greater_out)


def solution(mesh):
    in_specs = (
        P(None, "energy", "elem"),
        P(None, "energy", "elem"),
        P("elem", None, None, None),
        P("elem"),
    )
    out_specs = (P(None, "energy", "elem"), P(None, "energy", "elem"))
    return jax.shard_map(shards, mesh=mesh, in_specs=in_specs, out_specs=out_specs, check_vma=False)
```

```python
import functools
import math

import jax
import jax.numpy as jnp
import numpy as np
from jax import lax
from jax.experimental import pallas as pl
from jax.experimental.pallas import tpu as pltpu
from jax.sharding import PartitionSpec as P

BF16 = jnp.bfloat16
F32 = jnp.float32
VMEM_BYTES = 24 * 1024 * 1024


def fourier_tables(length):
    half = length // 2
    steps = np.arange(half)[:, None] * np.arange(length)[None, :] % length
    angle = steps * (2.0 * math.pi / length)
    sines = np.sin(angle)
    sines[0] = 1.0 - 2.0 * (np.arange(length) % 2)
    table = np.concatenate([np.cos(angle), sines], 0)

    def split(values):
        high = values.astype(np.float32).astype(jnp.bfloat16)
        low = (values - high.astype(np.float64)).astype(np.float32).astype(jnp.bfloat16)
        return np.stack([high, low])

    return split(table), split(table.T)


def pack_kernel(lesser_ref, greater_ref, out_ref):
    pieces, _, _, lanes = out_ref.shape
    width = lanes // 2
    for n in range(pieces):
        cols = slice(n * width, (n + 1) * width)
        out_ref[n] = jnp.concatenate([lesser_ref[:, :, cols], greater_ref[:, :, cols]], axis=-1)


def unpack_kernel(in_ref, lesser_ref, greater_ref):
    pieces, _, _, lanes = in_ref.shape
    width = lanes // 2
    per_tile = max(1, 128 // width)
    for first in range(0, pieces, per_tile):
        group = range(first, min(first + per_tile, pieces))
        cols = slice(first * width, (group[-1] + 1) * width)
        lesser_ref[:, :, cols] = jnp.concatenate([in_ref[n][:, :, :width] for n in group], axis=-1)
        greater_ref[:, :, cols] = jnp.concatenate([in_ref[n][:, :, width:] for n in group], axis=-1)


def one_hot(index_row, depth):
    rows = lax.broadcasted_iota(jnp.int32, (depth, index_row.shape[-1]), 0)
    return jnp.where(rows == index_row, 1.0, 0.0).astype(BF16)


def dot(a, b):
    return lax.dot_general(a, b, (((1,), (0,)), ((), ())), preferred_element_type=F32)


def rows_of(ref, part):
    blocks, _, energies, lanes = ref.shape
    return ref[:, part].reshape(blocks * energies, lanes)


def forward_sums(table_ref, signals):
    return dot(table_ref[0], signals) + dot(table_ref[1], signals)


def correlate(near, far, inverse_ref):
    half = near.shape[0] // 2
    length = near.shape[0]
    lanes = near.shape[1] // 2

    def parts(sums):
        return [sums[i * half : (i + 1) * half, j * lanes : (j + 1) * lanes] for i in range(2) for j in range(2)]

    a_re, a_im, b_re, b_im = parts(near)
    c_re, c_im, d_re, d_im = parts(far)
    first = lax.broadcasted_iota(jnp.int32, (half, lanes), 0) == 0
    ac_re, ac_im = a_re * c_re - a_im * c_im, a_re * c_im + a_im * c_re
    bd_re, bd_im = b_re * d_re - b_im * d_im, b_re * d_im + b_im * d_re
    u_re = jnp.where(first, 0.5 * ac_re, ac_re + bd_re)
    u_im = jnp.where(first, 0.5 * ac_im, ac_im + bd_im)
    v_re = jnp.where(first, 0.5 * bd_re, b_re * c_re - b_im * c_im - (a_re * d_re - a_im * d_im))
    v_im = jnp.where(first, 0.5 * bd_im, b_re * c_im + b_im * c_re - (a_re * d_im + a_im * d_re))
    top = jnp.concatenate([u_im, -u_re], axis=-1)
    bottom = jnp.concatenate([v_im, -v_re], axis=-1)
    products = jnp.concatenate([top, bottom], axis=0)
    high = products.astype(BF16)
    low = (products - high.astype(F32)).astype(BF16)
    back = dot(inverse_ref[0], high) + (dot(inverse_ref[0], low) + dot(inverse_ref[1], high))
    return (back * (2.0 / (length * math.sqrt(length)))).astype(BF16)


def correlate_kernel(index_ref, own_ref, far_ref, forward_ref, inverse_ref, out_ref):
    blocks, _, energies, lanes = own_ref.shape
    far = far_ref[...]
    own, partner = [], []
    for part in range(2):
        pick_far = one_hot(index_ref[part : part + 1, :], far.shape[-1])
        own.append(rows_of(own_ref, part))
        partner.append(dot(far, pick_far).astype(BF16))
    near = forward_sums(forward_ref, jnp.concatenate(own, axis=-1))
    result = correlate(near, forward_sums(forward_ref, jnp.concatenate(partner, axis=-1)), inverse_ref)
    for part in range(2):
        out_ref[:, part] = result[:, part * lanes : (part + 1) * lanes].reshape(blocks, energies, lanes)


def call(kernel, out_shape, flops, *args, scratch=()):
    outs = out_shape if isinstance(out_shape, (list, tuple)) else [out_shape]
    moved = sum(math.prod(v.shape) * v.dtype.itemsize for v in [*args, *outs])
    return pl.pallas_call(
        kernel,
        out_shape=out_shape,
        scratch_shapes=list(scratch),
        compiler_params=pltpu.CompilerParams(vmem_limit_bytes=VMEM_BYTES),
        cost_estimate=pl.CostEstimate(flops=flops, bytes_accessed=moved, transcendentals=0),
    )(*args)


def place():
    me = lax.axis_index("energy")
    return me // 2, me % 2


def split_kernel(lesser_ref, greater_ref, *out_refs):
    chip, _ = place()
    width = out_refs[0].shape[-1] // 2
    for j, out_ref in enumerate(out_refs):
        cols = pl.ds(pl.multiple_of((chip ^ j) * 2 * width, 2 * width), 2 * width)
        lesser, greater = lesser_ref[:, :, cols], greater_ref[:, :, cols]
        out_ref[0] = jnp.concatenate([lesser[..., :width], greater[..., :width]], axis=-1)
        out_ref[1] = jnp.concatenate([lesser[..., width:], greater[..., width:]], axis=-1)


def lane_row(lanes):
    return lax.broadcasted_iota(jnp.int32, (1, lanes), 1)


def row_list(lists_ref, piece, group, own):
    lists = lists_ref[piece]
    here = lax.broadcasted_iota(jnp.int32, lists.shape, 0) == group
    return jnp.sum(jnp.where(here == own, lists, 0), axis=0, keepdims=True)


def outgoing_kernel(lists_ref, *refs):
    in_refs, (first_ref, second_ref, sibling_ref) = refs[:4], refs[4:]
    chip, core = place()
    group = lax.axis_index("elem")
    energies, lanes = first_ref.shape[1:]
    cap = lanes // 4
    lane = lane_row(lanes)
    for which, out_ref in enumerate((first_ref, second_ref)):
        rows = row_list(lists_ref, 2 * chip + which, group, False)
        rows = rows + jnp.where(lane // cap % 2 == 1, lanes // 2, 0)
        total = None
        for part in range(2):
            values = jnp.concatenate([ref[which, part] for ref in in_refs], axis=0)
            picked = dot(values, one_hot(jnp.where(lane // (2 * cap) == part, rows, -1), lanes))
            total = picked if total is None else total + picked
        out_ref[...] = total.astype(BF16).reshape(4, energies, lanes)
    for j, ref in enumerate(in_refs):
        sibling_ref[j] = ref[1 - core]


def exchange_kernel(lists_ref, slots_ref, *refs):
    in_refs, (sibling_ref, far_ref, far_sibling_ref, forward_ref, inverse_ref) = refs[:4], refs[4:9]
    out_refs, (own, far) = refs[9:13], refs[13:]
    chip, core = place()
    group = lax.axis_index("elem")
    energies, lanes = far_ref.shape[1:]
    width, cap = lanes // 2, lanes // 4
    for j, ref in enumerate(in_refs):
        here = pl.ds(pl.multiple_of((2 * (chip ^ j) + core) * energies, energies), energies)
        there = pl.ds(pl.multiple_of((2 * (chip ^ j) + 1 - core) * energies, energies), energies)
        for part in range(2):
            cols = slice(part * lanes, (part + 1) * lanes)
            own[here, cols] = ref[core, part]
            own[there, cols] = sibling_ref[j, part]
        far[here, :] = far_ref[j]
        far[there, :] = far_sibling_ref[j]
    piece = 2 * chip + core
    lane = lane_row(lanes)
    slots = slots_ref[pl.ds(piece, 1), :]
    source = slots // cap
    spot = slots - source * cap + jnp.where(lane < width, cap, 0)
    rows = row_list(lists_ref, piece, group, True) + jnp.where(lane // cap % 2 == 1, width, 0)
    chosen = one_hot(jnp.where(lane < 2 * cap, rows, -1), lanes)
    pick_own = dot(chosen, one_hot(jnp.where(source == group, spot, -1), lanes)).astype(BF16)
    cross = far[...]
    partner = []
    for part in range(2):
        pick_far = one_hot(jnp.where(source == group, -1, spot + 2 * cap * part), lanes)
        both = dot(own[:, part * lanes : (part + 1) * lanes], pick_own) + dot(cross, pick_far)
        partner.append(both.astype(BF16))
    near = forward_sums(forward_ref, own[...])
    result = correlate(near, forward_sums(forward_ref, jnp.concatenate(partner, axis=-1)), inverse_ref)
    own[...] = result
    for j, ref in enumerate(out_refs):
        for which in range(2):
            here = pl.ds(pl.multiple_of((2 * (chip ^ j) + which) * energies, energies), energies)
            for part in range(2):
                ref[which, part] = own[here, part * lanes : (part + 1) * lanes]


def join_kernel(*refs):
    in_refs, sibling_refs, (lesser_ref, greater_ref) = refs[:4], refs[4:8], refs[8:]
    chip, core = place()
    width = in_refs[0].shape[-1] // 2
    for j in range(4):
        mine, other = in_refs[j][core], sibling_refs[j][core]
        even = jnp.where(core == 0, mine, other)
        odd = jnp.where(core == 0, other, mine)
        cols = pl.ds(pl.multiple_of((chip ^ j) * 2 * width, 2 * width), 2 * width)
        lesser_ref[:, :, cols] = jnp.concatenate([even[..., :width], odd[..., :width]], axis=-1)
        greater_ref[:, :, cols] = jnp.concatenate([even[..., width:], odd[..., width:]], axis=-1)


def swap(values, axis, bit):
    return lax.ppermute(values, axis, [(i, i ^ bit) for i in range(lax.axis_size(axis))])


def over_chips(values):
    return [values[0]] + [swap(values[j], "energy", 2 * j) for j in range(1, 4)]


def four_chips(g_lesser, g_greater, send_rows, partner_slot):
    chip, core = place()
    group = lax.axis_index("elem")
    _, energies, group_rows = g_lesser.shape
    groups, cap = send_rows.shape[2:]
    lanes = 4 * cap
    length = 8 * energies
    pair = jax.ShapeDtypeStruct((2, 2, energies, lanes), BF16)
    quarter = jax.ShapeDtypeStruct((4, energies, lanes), BF16)
    sibling = jax.ShapeDtypeStruct((4, 2, energies, lanes), BF16)

    lists = jnp.tile(send_rows[0], (1, 1, 4))
    slots = jnp.tile(partner_slot.reshape(8, lanes // 2), (1, 2))
    ids = jnp.arange(groups, dtype=jnp.int32)
    filled = jnp.sum(send_rows[0], axis=2) > 0
    flips = jnp.sum(jnp.where(filled, (ids ^ group)[None, :], 0), axis=1)
    flip_first = lax.dynamic_index_in_dim(flips, 2 * chip, 0, keepdims=False)
    flip_second = lax.dynamic_index_in_dim(flips, 2 * chip + 1, 0, keepdims=False)

    arrived = over_chips(call(split_kernel, [pair] * 4, 0, g_lesser, g_greater))
    first, second, for_sibling = call(outgoing_kernel, [quarter, quarter, sibling], 2**26, lists, *arrived)
    first_one, second_one = swap(first, "elem", 1), swap(second, "elem", 2)
    from_sibling = swap(for_sibling, "energy", 1)
    first_two = swap(jnp.where(flip_first == 3, first_one, first), "elem", 2)
    second_two = swap(jnp.where(flip_second == 3, second_one, second), "elem", 1)
    first = jnp.where(flip_first == 1, first_one, first_two)
    second = jnp.where(flip_second == 2, second_one, second_two)
    far_sibling = swap(jnp.where(core == 0, second, first), "energy", 1)
    far = jnp.where(core == 0, first, second)
    forward, inverse = fourier_tables(length)
    results = call(
        exchange_kernel,
        [pair] * 4,
        2 * length * length * lanes * 14,
        lists,
        slots,
        *arrived,
        from_sibling,
        far,
        far_sibling,
        jnp.asarray(forward),
        jnp.asarray(inverse),
        scratch=[pltpu.VMEM((length, 2 * lanes), BF16), pltpu.VMEM((length, lanes), BF16)],
    )
    back = over_chips(results)
    back_sibling = [swap(values, "energy", 1) for values in back]
    out = jax.ShapeDtypeStruct((2, energies, group_rows), BF16)
    return tuple(call(join_kernel, [out, out], 0, *back, *back_sibling))


def any_mesh(g_lesser, g_greater, send_rows, partner_slot):
    piece = lax.axis_index("energy")
    pieces = lax.axis_size("energy")
    _, energies, group_rows = g_lesser.shape
    groups, cap = send_rows.shape[2:]
    width = group_rows // pieces
    lanes = 2 * width
    length = pieces * energies
    packed_shape = jax.ShapeDtypeStruct((pieces, 2, energies, lanes), BF16)
    packed = call(pack_kernel, packed_shape, 0, g_lesser, g_greater)
    own = lax.all_to_all(packed, "energy", split_axis=0, concat_axis=0, tiled=True)
    rows = lax.dynamic_index_in_dim(send_rows[0], piece, 0, keepdims=False).reshape(-1)
    slots = lax.dynamic_slice_in_dim(partner_slot, piece * width, width, 0)
    pick = (jnp.arange(width, dtype=jnp.int32)[:, None] == rows[None, :]).astype(BF16)
    split = own.reshape(pieces, 2, energies, 2, width)
    outgoing = jnp.einsum("pceds,sm->mpced", split, pick, preferred_element_type=F32).astype(BF16)
    incoming = lax.all_to_all(outgoing, "elem", split_axis=0, concat_axis=0, tiled=True)
    table_width = groups * cap
    far = jnp.transpose(incoming, (1, 3, 2, 4, 0)).reshape(length, 4 * table_width)
    index = jnp.concatenate([slots + table_width, slots])
    index = jnp.stack([index, index + 2 * table_width])
    forward, inverse = fourier_tables(length)
    result = call(
        correlate_kernel,
        packed_shape,
        2 * length * length * lanes * 14,
        index,
        own,
        far,
        jnp.asarray(forward),
        jnp.asarray(inverse),
    )
    back = lax.all_to_all(result, "energy", split_axis=0, concat_axis=0, tiled=True)
    out = jax.ShapeDtypeStruct((2, energies, group_rows), BF16)
    return tuple(call(unpack_kernel, [out, out], 0, back))


def shards(g_lesser, g_greater, send_rows, partner_slot):
    _, pieces, groups, cap = send_rows.shape
    fits = pieces == 8 and groups == 4 and cap == 32 and partner_slot.shape[0] == 512
    path = four_chips if fits else any_mesh
    return path(g_lesser, g_greater, send_rows, partner_slot)


def solution(mesh):
    in_specs = (
        P(None, "energy", "elem"),
        P(None, "energy", "elem"),
        P("elem", None, None, None),
        P("elem"),
    )
    out_specs = (P(None, "energy", "elem"), P(None, "energy", "elem"))
    return jax.shard_map(shards, mesh=mesh, in_specs=in_specs, out_specs=out_specs, check_vma=False)
```

```python
import functools
import math

import jax
import jax.numpy as jnp
import numpy as np
from jax import lax
from jax.experimental import pallas as pl
from jax.experimental.pallas import tpu as pltpu
from jax.sharding import PartitionSpec as P

BF16 = jnp.bfloat16
F32 = jnp.float32
VMEM_BYTES = 24 * 1024 * 1024


def fourier_tables(length):
    half = length // 2
    steps = np.arange(half)[:, None] * np.arange(length)[None, :] % length
    angle = steps * (2.0 * math.pi / length)
    sines = np.sin(angle)
    sines[0] = 1.0 - 2.0 * (np.arange(length) % 2)
    table = np.concatenate([np.cos(angle), sines], 0)

    def split(values):
        high = values.astype(np.float32).astype(jnp.bfloat16)
        low = (values - high.astype(np.float64)).astype(np.float32).astype(jnp.bfloat16)
        return np.stack([high, low])

    return np.concatenate([split(table), split(table.T)])


def pack_kernel(lesser_ref, greater_ref, out_ref):
    pieces, _, _, lanes = out_ref.shape
    width = lanes // 2
    for n in range(pieces):
        cols = slice(n * width, (n + 1) * width)
        out_ref[n] = jnp.concatenate([lesser_ref[:, :, cols], greater_ref[:, :, cols]], axis=-1)


def unpack_kernel(in_ref, lesser_ref, greater_ref):
    pieces, _, _, lanes = in_ref.shape
    width = lanes // 2
    per_tile = max(1, 128 // width)
    for first in range(0, pieces, per_tile):
        group = range(first, min(first + per_tile, pieces))
        cols = slice(first * width, (group[-1] + 1) * width)
        lesser_ref[:, :, cols] = jnp.concatenate([in_ref[n][:, :, :width] for n in group], axis=-1)
        greater_ref[:, :, cols] = jnp.concatenate([in_ref[n][:, :, width:] for n in group], axis=-1)


def one_hot(index_row, depth):
    rows = lax.broadcasted_iota(jnp.int32, (depth, index_row.shape[-1]), 0)
    return jnp.where(rows == index_row, 1.0, 0.0).astype(BF16)


def dot(a, b):
    return lax.dot_general(a, b, (((1,), (0,)), ((), ())), preferred_element_type=F32)


def rows_of(ref, part):
    blocks, _, energies, lanes = ref.shape
    return ref[:, part].reshape(blocks * energies, lanes)


def forward_sums(table_ref, signals):
    return dot(table_ref[0], signals) + dot(table_ref[1], signals)


def correlate(near, far, table_ref):
    half = near.shape[0] // 2
    length = near.shape[0]
    lanes = near.shape[1] // 2

    def parts(sums):
        return [sums[i * half : (i + 1) * half, j * lanes : (j + 1) * lanes] for i in range(2) for j in range(2)]

    a_re, a_im, b_re, b_im = parts(near)
    c_re, c_im, d_re, d_im = parts(far)
    first = lax.broadcasted_iota(jnp.int32, (half, lanes), 0) == 0
    ac_re, ac_im = a_re * c_re - a_im * c_im, a_re * c_im + a_im * c_re
    bd_re, bd_im = b_re * d_re - b_im * d_im, b_re * d_im + b_im * d_re
    u_re = jnp.where(first, 0.5 * ac_re, ac_re + bd_re)
    u_im = jnp.where(first, 0.5 * ac_im, ac_im + bd_im)
    v_re = jnp.where(first, 0.5 * bd_re, b_re * c_re - b_im * c_im - (a_re * d_re - a_im * d_im))
    v_im = jnp.where(first, 0.5 * bd_im, b_re * c_im + b_im * c_re - (a_re * d_im + a_im * d_re))
    top = jnp.concatenate([u_im, -u_re], axis=-1)
    bottom = jnp.concatenate([v_im, -v_re], axis=-1)
    products = jnp.concatenate([top, bottom], axis=0)
    high = products.astype(BF16)
    low = (products - high.astype(F32)).astype(BF16)
    back = dot(table_ref[2], high) + (dot(table_ref[2], low) + dot(table_ref[3], high))
    return (back * (2.0 / (length * math.sqrt(length)))).astype(BF16)


def correlate_kernel(index_ref, own_ref, far_ref, table_ref, out_ref):
    blocks, _, energies, lanes = own_ref.shape
    far = far_ref[...]
    own, partner = [], []
    for part in range(2):
        pick_far = one_hot(index_ref[part : part + 1, :], far.shape[-1])
        own.append(rows_of(own_ref, part))
        partner.append(dot(far, pick_far).astype(BF16))
    near = forward_sums(table_ref, jnp.concatenate(own, axis=-1))
    result = correlate(near, forward_sums(table_ref, jnp.concatenate(partner, axis=-1)), table_ref)
    for part in range(2):
        out_ref[:, part] = result[:, part * lanes : (part + 1) * lanes].reshape(blocks, energies, lanes)


def call(kernel, out_shape, flops, *args, scratch=(), in_hbm=False):
    outs = out_shape if isinstance(out_shape, (list, tuple)) else [out_shape]
    moved = sum(math.prod(v.shape) * v.dtype.itemsize for v in [*args, *outs])
    more = {"in_specs": [pl.BlockSpec(memory_space=pltpu.HBM)] * len(args)} if in_hbm else {}
    return pl.pallas_call(
        kernel,
        out_shape=out_shape,
        scratch_shapes=list(scratch),
        compiler_params=pltpu.CompilerParams(vmem_limit_bytes=VMEM_BYTES),
        cost_estimate=pl.CostEstimate(flops=flops, bytes_accessed=moved, transcendentals=0),
        **more,
    )(*args)


def place():
    me = lax.axis_index("energy")
    return me // 2, me % 2


def columns_of(chip, width):
    return pl.ds(pl.multiple_of(chip * 2 * width, 2 * width), 2 * width)


def split_kernel(lesser_ref, greater_ref, *refs):
    (diagonal_ref, beside_ref, keep_ref, give_ref, own_ref), (held, sems) = refs[:5], refs[5:]
    chip, core = place()
    width = own_ref.shape[-1] // 2
    copies = [
        [
            pltpu.make_async_copy(ref.at[:, :, columns_of(chip ^ j, width)], held.at[j, i], sems.at[j, i])
            for i, ref in enumerate((lesser_ref, greater_ref))
        ]
        for j in range(4)
    ]
    for j in (3, 2, 1, 0):
        for copy in copies[j]:
            copy.start()
    for j in (3, 2, 1, 0):
        for copy in copies[j]:
            copy.wait()
        lesser, greater = held[j, 0], held[j, 1]
        zero = jnp.concatenate([lesser[..., :width], greater[..., :width]], axis=-1)
        one = jnp.concatenate([lesser[..., width:], greater[..., width:]], axis=-1)
        if j >= 2:
            out_ref = diagonal_ref if j == 3 else beside_ref
            out_ref[0], out_ref[1] = zero, one
        else:
            keep = keep_ref if j == 1 else own_ref
            keep[...] = jnp.where(core == 0, zero, one)
            give_ref[1 - j] = jnp.where(core == 0, one, zero)


def swap(values, axis, bit):
    return lax.ppermute(values, axis, [(i, i ^ bit) for i in range(lax.axis_size(axis))])


def over_energy(diagonal, beside, keep, give, own):
    diagonal = swap(diagonal, "energy", 6)
    beside = swap(beside, "energy", 4)
    got = swap(give, "energy", 1)
    across = swap(jnp.stack([keep, got[0]]), "energy", 2)
    return own, got, across, beside, swap(beside, "energy", 1), diagonal, swap(diagonal, "energy", 1)


def blocks_of(refs, core):
    own_ref, got_ref, across_ref, beside_ref, beside_other_ref, diagonal_ref, diagonal_other_ref = refs
    return [
        (lambda: own_ref[...], lambda: got_ref[1]),
        (lambda: across_ref[0], lambda: across_ref[1]),
        (lambda: beside_ref[core], lambda: beside_other_ref[core]),
        (lambda: diagonal_ref[core], lambda: diagonal_other_ref[core]),
    ]


def lane_row(lanes):
    return lax.broadcasted_iota(jnp.int32, (1, lanes), 1)


def energies_of(device, energies):
    return pl.ds(pl.multiple_of(device * energies, energies), energies)


def gather_kernel(lists_ref, slots_ref, *refs):
    in_refs, (signals_ref, first_ref, second_ref, picks_ref, flip_ref) = refs[:7], refs[7:]
    chip, core = place()
    group = lax.axis_index("elem")
    energies, lanes = in_refs[0].shape[1:]
    width, cap = lanes // 2, lanes // 4
    for j, pair in enumerate(blocks_of(in_refs, core)):
        for which, block in enumerate(pair):
            values = block()
            rows = energies_of(2 * (chip ^ j) + (core if which == 0 else 1 - core), energies)
            for part in range(2):
                signals_ref[rows, part * lanes : (part + 1) * lanes] = values[part]
    piece = 2 * chip + core
    lane = lane_row(lanes)
    lists = lists_ref[piece]
    ids = lax.broadcasted_iota(jnp.int32, lists.shape, 0)
    greater = jnp.where(lane // cap % 2 == 1, width, 0)
    near_rows = jnp.sum(jnp.where(ids == group, lists, 0), axis=0, keepdims=True) + greater
    far_rows = jnp.sum(jnp.where(ids == group, 0, lists), axis=0, keepdims=True) + greater
    filled = jnp.max(lists, axis=1, keepdims=True) > 0
    flip = jnp.sum(jnp.where(filled, ids ^ group, 0), axis=0, keepdims=True)
    flip_ref[...] = jnp.broadcast_to(flip, flip_ref.shape)
    total = None
    for part in range(2):
        pick = one_hot(jnp.where(lane // (2 * cap) == part, far_rows, -1), lanes)
        picked = dot(signals_ref[:, part * lanes : (part + 1) * lanes], pick)
        total = picked if total is None else total + picked
    half = first_ref.shape[0]
    first_ref[...] = total[:half].astype(BF16)
    second_ref[...] = total[half:].astype(BF16)
    slots = slots_ref[pl.ds(piece, 1), :]
    source = slots // cap
    spot = slots - source * cap + jnp.where(lane < width, cap, 0)
    near = one_hot(jnp.where(lane < 2 * cap, near_rows, -1), lanes)
    picks_ref[0] = dot(near, one_hot(jnp.where(source == group, spot, -1), lanes)).astype(BF16)
    for part in range(2):
        picks_ref[1 + part] = one_hot(jnp.where(source == group, -1, spot + 2 * cap * part), lanes)


def own_kernel(signals_ref, picks_ref, table_ref, near_ref, partner_ref):
    lanes = picks_ref.shape[-1]
    for part in range(2):
        cols = slice(part * lanes, (part + 1) * lanes)
        partner_ref[:, cols] = dot(signals_ref[:, cols], picks_ref[0]).astype(BF16)
    near_ref[...] = forward_sums(table_ref, signals_ref[...])


def exchange_kernel(flip_ref, near_ref, partner_ref, picks_ref, first_ref, first_far_ref, second_ref, second_far_ref, table_ref, *refs):
    (diagonal_ref, beside_ref, keep_ref, give_ref, own_ref), (held,) = refs[:5], refs[5:]
    chip, core = place()
    energies, lanes = own_ref.shape[1:]
    flip = flip_ref[0:1, :]
    far = jnp.concatenate(
        [
            jnp.where(flip == 1, first_ref[...], first_far_ref[...]),
            jnp.where(flip == 2, second_ref[...], second_far_ref[...]),
        ],
        axis=0,
    )
    partner = [
        (partner_ref[:, part * lanes : (part + 1) * lanes].astype(F32) + dot(far, picks_ref[1 + part])).astype(BF16)
        for part in range(2)
    ]
    held[...] = correlate(near_ref[...], forward_sums(table_ref, jnp.concatenate(partner, axis=-1)), table_ref)

    def block(device):
        rows = energies_of(device, energies)
        return [held[rows, part * lanes : (part + 1) * lanes] for part in range(2)]

    for j, ref in ((3, diagonal_ref), (2, beside_ref)):
        for which in range(2):
            for part, values in enumerate(block(2 * (chip ^ j) + which)):
                ref[which, part] = values
    for j, ref in ((1, keep_ref), (0, own_ref)):
        for part, values in enumerate(block(2 * (chip ^ j) + core)):
            ref[part] = values
        for part, values in enumerate(block(2 * (chip ^ j) + 1 - core)):
            give_ref[1 - j, part] = values


def join_kernel(*refs):
    in_refs, (lesser_ref, greater_ref) = refs[:7], refs[7:]
    chip, core = place()
    width = in_refs[0].shape[-1] // 2
    for j, (mine, other) in enumerate(blocks_of(in_refs, core)):
        mine, other = mine(), other()
        even = jnp.where(core == 0, mine, other)
        odd = jnp.where(core == 0, other, mine)
        cols = columns_of(chip ^ j, width)
        lesser_ref[:, :, cols] = jnp.concatenate([even[..., :width], odd[..., :width]], axis=-1)
        greater_ref[:, :, cols] = jnp.concatenate([even[..., width:], odd[..., width:]], axis=-1)


def four_chips(g_lesser, g_greater, send_rows, partner_slot):
    _, energies, group_rows = g_lesser.shape
    cap = send_rows.shape[-1]
    lanes = 4 * cap
    length = 8 * energies
    block = jax.ShapeDtypeStruct((2, energies, lanes), BF16)
    pair = jax.ShapeDtypeStruct((2, 2, energies, lanes), BF16)
    leaving = [pair, pair, block, pair, block]
    half = jax.ShapeDtypeStruct((length // 2, lanes), BF16)
    whole = jax.ShapeDtypeStruct((length, 2 * lanes), BF16)
    lists = jnp.tile(send_rows[0], (1, 1, 4))
    slots = jnp.tile(partner_slot.reshape(8, lanes // 2), (1, 2))
    table = jnp.asarray(fourier_tables(length))

    scratch = [pltpu.VMEM((4, 2, 2, energies, lanes), BF16), pltpu.SemaphoreType.DMA((4, 2))]
    packed = call(split_kernel, leaving, 0, g_lesser, g_greater, scratch=scratch, in_hbm=True)
    arrived = over_energy(*packed)
    gathered = [whole, half, half, jax.ShapeDtypeStruct((3, lanes, lanes), BF16), jax.ShapeDtypeStruct((8, lanes), jnp.int32)]
    signals, first, second, picks, flip = call(gather_kernel, gathered, 2**26, lists, slots, *arrived)
    relay = flip[:1] == 3
    first_one, second_one = swap(first, "elem", 1), swap(second, "elem", 2)
    sums = jax.ShapeDtypeStruct((length, 2 * lanes), F32)
    near, partner = call(own_kernel, [sums, whole], 2**29, signals, picks, table)
    first_two = swap(jnp.where(relay, first_one, first), "elem", 2)
    second_two = swap(jnp.where(relay, second_one, second), "elem", 1)
    results = call(
        exchange_kernel,
        leaving,
        2**30,
        flip,
        near,
        partner,
        picks,
        first_one,
        first_two,
        second_one,
        second_two,
        table,
        scratch=[pltpu.VMEM((length, 2 * lanes), BF16)],
    )
    out = jax.ShapeDtypeStruct((2, energies, group_rows), BF16)
    return tuple(call(join_kernel, [out, out], 0, *over_energy(*results)))


def any_mesh(g_lesser, g_greater, send_rows, partner_slot):
    piece = lax.axis_index("energy")
    pieces = lax.axis_size("energy")
    _, energies, group_rows = g_lesser.shape
    groups, cap = send_rows.shape[2:]
    width = group_rows // pieces
    lanes = 2 * width
    length = pieces * energies
    packed_shape = jax.ShapeDtypeStruct((pieces, 2, energies, lanes), BF16)
    packed = call(pack_kernel, packed_shape, 0, g_lesser, g_greater)
    own = lax.all_to_all(packed, "energy", split_axis=0, concat_axis=0, tiled=True)
    rows = lax.dynamic_index_in_dim(send_rows[0], piece, 0, keepdims=False).reshape(-1)
    slots = lax.dynamic_slice_in_dim(partner_slot, piece * width, width, 0)
    pick = (jnp.arange(width, dtype=jnp.int32)[:, None] == rows[None, :]).astype(BF16)
    split = own.reshape(pieces, 2, energies, 2, width)
    outgoing = jnp.einsum("pceds,sm->mpced", split, pick, preferred_element_type=F32).astype(BF16)
    incoming = lax.all_to_all(outgoing, "elem", split_axis=0, concat_axis=0, tiled=True)
    table_width = groups * cap
    far = jnp.transpose(incoming, (1, 3, 2, 4, 0)).reshape(length, 4 * table_width)
    index = jnp.concatenate([slots + table_width, slots])
    index = jnp.stack([index, index + 2 * table_width])
    result = call(
        correlate_kernel,
        packed_shape,
        2 * length * length * lanes * 14,
        index,
        own,
        far,
        jnp.asarray(fourier_tables(length)),
    )
    back = lax.all_to_all(result, "energy", split_axis=0, concat_axis=0, tiled=True)
    out = jax.ShapeDtypeStruct((2, energies, group_rows), BF16)
    return tuple(call(unpack_kernel, [out, out], 0, back))


def shards(g_lesser, g_greater, send_rows, partner_slot):
    _, pieces, groups, cap = send_rows.shape
    fits = pieces == 8 and groups == 4 and cap == 32 and partner_slot.shape[0] == 512
    path = four_chips if fits else any_mesh
    return path(g_lesser, g_greater, send_rows, partner_slot)


def solution(mesh):
    in_specs = (
        P(None, "energy", "elem"),
        P(None, "energy", "elem"),
        P("elem", None, None, None),
        P("elem"),
    )
    out_specs = (P(None, "energy", "elem"), P(None, "energy", "elem"))
    return jax.shard_map(shards, mesh=mesh, in_specs=in_specs, out_specs=out_specs, check_vma=False)
```

```python
import functools
import math

import jax
import jax.numpy as jnp
import numpy as np
from jax import lax
from jax.experimental import pallas as pl
from jax.experimental.pallas import tpu as pltpu
from jax.sharding import PartitionSpec as P

BF16 = jnp.bfloat16
F32 = jnp.float32
VMEM_BYTES = 24 * 1024 * 1024


def fourier_tables(length):
    half = length // 2
    steps = np.arange(half)[:, None] * np.arange(length)[None, :] % length
    angle = steps * (2.0 * math.pi / length)
    sines = np.sin(angle)
    sines[0] = 1.0 - 2.0 * (np.arange(length) % 2)
    table = np.concatenate([np.cos(angle), sines], 0)

    def split(values):
        high = values.astype(np.float32).astype(jnp.bfloat16)
        low = (values - high.astype(np.float64)).astype(np.float32).astype(jnp.bfloat16)
        return np.stack([high, low])

    return np.concatenate([split(table), split(table.T)])


def pack_kernel(lesser_ref, greater_ref, out_ref):
    pieces, _, _, lanes = out_ref.shape
    width = lanes // 2
    for n in range(pieces):
        cols = slice(n * width, (n + 1) * width)
        out_ref[n] = jnp.concatenate([lesser_ref[:, :, cols], greater_ref[:, :, cols]], axis=-1)


def unpack_kernel(in_ref, lesser_ref, greater_ref):
    pieces, _, _, lanes = in_ref.shape
    width = lanes // 2
    per_tile = max(1, 128 // width)
    for first in range(0, pieces, per_tile):
        group = range(first, min(first + per_tile, pieces))
        cols = slice(first * width, (group[-1] + 1) * width)
        lesser_ref[:, :, cols] = jnp.concatenate([in_ref[n][:, :, :width] for n in group], axis=-1)
        greater_ref[:, :, cols] = jnp.concatenate([in_ref[n][:, :, width:] for n in group], axis=-1)


def one_hot(index_row, depth):
    rows = lax.broadcasted_iota(jnp.int32, (depth, index_row.shape[-1]), 0)
    return jnp.where(rows == index_row, 1.0, 0.0).astype(BF16)


def dot(a, b):
    return lax.dot_general(a, b, (((1,), (0,)), ((), ())), preferred_element_type=F32)


def rows_of(ref, part):
    blocks, _, energies, lanes = ref.shape
    return ref[:, part].reshape(blocks * energies, lanes)


def forward_sums(table_ref, signals):
    return dot(table_ref[0], signals) + dot(table_ref[1], signals)


def correlate(near, far, table_ref):
    half = near.shape[0] // 2
    length = near.shape[0]
    lanes = near.shape[1] // 2

    def parts(sums):
        return [sums[i * half : (i + 1) * half, j * lanes : (j + 1) * lanes] for i in range(2) for j in range(2)]

    a_re, a_im, b_re, b_im = parts(near)
    c_re, c_im, d_re, d_im = parts(far)
    first = lax.broadcasted_iota(jnp.int32, (half, lanes), 0) == 0
    ac_re, ac_im = a_re * c_re - a_im * c_im, a_re * c_im + a_im * c_re
    bd_re, bd_im = b_re * d_re - b_im * d_im, b_re * d_im + b_im * d_re
    u_re = jnp.where(first, 0.5 * ac_re, ac_re + bd_re)
    u_im = jnp.where(first, 0.5 * ac_im, ac_im + bd_im)
    v_re = jnp.where(first, 0.5 * bd_re, b_re * c_re - b_im * c_im - (a_re * d_re - a_im * d_im))
    v_im = jnp.where(first, 0.5 * bd_im, b_re * c_im + b_im * c_re - (a_re * d_im + a_im * d_re))
    top = jnp.concatenate([u_im, -u_re], axis=-1)
    bottom = jnp.concatenate([v_im, -v_re], axis=-1)
    products = jnp.concatenate([top, bottom], axis=0)
    high = products.astype(BF16)
    low = (products - high.astype(F32)).astype(BF16)
    back = dot(table_ref[2], high) + (dot(table_ref[2], low) + dot(table_ref[3], high))
    return (back * (2.0 / (length * math.sqrt(length)))).astype(BF16)


def correlate_kernel(index_ref, own_ref, far_ref, table_ref, out_ref):
    blocks, _, energies, lanes = own_ref.shape
    far = far_ref[...]
    own, partner = [], []
    for part in range(2):
        pick_far = one_hot(index_ref[part : part + 1, :], far.shape[-1])
        own.append(rows_of(own_ref, part))
        partner.append(dot(far, pick_far).astype(BF16))
    near = forward_sums(table_ref, jnp.concatenate(own, axis=-1))
    result = correlate(near, forward_sums(table_ref, jnp.concatenate(partner, axis=-1)), table_ref)
    for part in range(2):
        out_ref[:, part] = result[:, part * lanes : (part + 1) * lanes].reshape(blocks, energies, lanes)


def call(kernel, out_shape, flops, *args, scratch=(), in_hbm=False):
    outs = out_shape if isinstance(out_shape, (list, tuple)) else [out_shape]
    moved = sum(math.prod(v.shape) * v.dtype.itemsize for v in [*args, *outs])
    more = {"in_specs": [pl.BlockSpec(memory_space=pltpu.HBM)] * len(args)} if in_hbm else {}
    if in_hbm:
        args = [pltpu.with_memory_space_constraint(v, pltpu.HBM) for v in args]
    return pl.pallas_call(
        kernel,
        out_shape=out_shape,
        scratch_shapes=list(scratch),
        compiler_params=pltpu.CompilerParams(vmem_limit_bytes=VMEM_BYTES),
        cost_estimate=pl.CostEstimate(flops=flops, bytes_accessed=moved, transcendentals=0),
        **more,
    )(*args)


def place():
    me = lax.axis_index("energy")
    return me // 2, me % 2


def columns_of(chip, width):
    return pl.ds(pl.multiple_of(chip * 2 * width, 2 * width), 2 * width)


def split_kernel(lists_ref, slots_ref, lesser_ref, greater_ref, *refs):
    (diagonal_ref, beside_ref, keep_ref, give_ref, own_ref, picks_ref, flip_ref) = refs[:7]
    held, lists, slots, sems, index_sems = refs[7:]
    chip, core = place()
    index_copies = [
        pltpu.make_async_copy(lists_ref.at[0, 2 * chip + core], lists, index_sems.at[0]),
        pltpu.make_async_copy(slots_ref, slots, index_sems.at[1]),
    ]
    for copy in index_copies:
        copy.start()
    width = own_ref.shape[-1] // 2
    copies = [
        [
            pltpu.make_async_copy(ref.at[:, :, columns_of(chip ^ j, width)], held.at[j, i], sems.at[j, i])
            for i, ref in enumerate((lesser_ref, greater_ref))
        ]
        for j in range(4)
    ]
    for j in (3, 2, 1, 0):
        for copy in copies[j]:
            copy.start()
    for copy in index_copies:
        copy.wait()
    index_tables(lists[...], slots[pl.ds(chip, 1), :], picks_ref, flip_ref)
    for j in (3, 2, 1, 0):
        for copy in copies[j]:
            copy.wait()
        lesser, greater = held[j, 0], held[j, 1]
        zero = jnp.concatenate([lesser[..., :width], greater[..., :width]], axis=-1)
        one = jnp.concatenate([lesser[..., width:], greater[..., width:]], axis=-1)
        if j >= 2:
            out_ref = diagonal_ref if j == 3 else beside_ref
            out_ref[0], out_ref[1] = zero, one
        else:
            keep = keep_ref if j == 1 else own_ref
            keep[...] = jnp.where(core == 0, zero, one)
            give_ref[1 - j] = jnp.where(core == 0, one, zero)


def swap(values, axis, bit):
    return lax.ppermute(values, axis, [(i, i ^ bit) for i in range(lax.axis_size(axis))])


def over_energy(diagonal, beside, keep, give, own):
    diagonal = swap(diagonal, "energy", 6)
    beside = swap(beside, "energy", 4)
    got = swap(give, "energy", 1)
    across = swap(jnp.stack([keep, got[0]]), "energy", 2)
    return own, got, diagonal, swap(diagonal, "energy", 1), beside, swap(beside, "energy", 1), across


def blocks_of(refs, core):
    own_ref, got_ref, diagonal_ref, diagonal_other_ref, beside_ref, beside_other_ref, across_ref = refs
    return [
        (lambda: own_ref[...], lambda: got_ref[1]),
        (lambda: across_ref[0], lambda: across_ref[1]),
        (lambda: beside_ref[core], lambda: beside_other_ref[core]),
        (lambda: diagonal_ref[core], lambda: diagonal_other_ref[core]),
    ]


def lane_row(lanes):
    return lax.broadcasted_iota(jnp.int32, (1, lanes), 1)


def energies_of(device, energies):
    return pl.ds(pl.multiple_of(device * energies, energies), energies)


def repeat(values, index_row):
    return dot(values.astype(F32).astype(BF16), one_hot(index_row, values.shape[-1])).astype(jnp.int32)


def relay_kernel(flip_ref, passed_ref, own_ref, out_ref):
    out_ref[...] = jnp.where(flip_ref[0:1, :] == 3, passed_ref[...], own_ref[...])


def index_tables(lists, slots, picks_ref, flip_ref):
    _, core = place()
    group = lax.axis_index("elem")
    lanes = picks_ref.shape[-1]
    width, cap = lanes // 2, lanes // 4
    lane = lane_row(lanes)
    lists = repeat(lists, lane % cap)
    ids = lax.broadcasted_iota(jnp.int32, lists.shape, 0)
    greater = jnp.where(lane // cap % 2 == 1, width, 0)
    near_rows = jnp.sum(jnp.where(ids == group, lists, 0), axis=0, keepdims=True) + greater
    far_rows = jnp.sum(jnp.where(ids == group, 0, lists), axis=0, keepdims=True) + greater
    filled = jnp.max(lists, axis=1, keepdims=True) > 0
    flip = jnp.sum(jnp.where(filled, ids ^ group, 0), axis=0, keepdims=True)
    flip_ref[...] = jnp.broadcast_to(flip[:, :1], flip_ref.shape)
    slots = repeat(slots, core * width + lane % width)
    source = slots // cap
    spot = slots - source * cap + jnp.where(lane < width, cap, 0)
    near = one_hot(jnp.where(lane < 2 * cap, near_rows, -1), lanes)
    picks_ref[0] = dot(near, one_hot(jnp.where(source == group, spot, -1), lanes)).astype(BF16)
    for part in range(2):
        picks_ref[1 + part] = one_hot(jnp.where(source == group, -1, spot + 2 * cap * part), lanes)
        picks_ref[3 + part] = one_hot(jnp.where(lane // (2 * cap) == part, far_rows, -1), lanes)


def gather_kernel(picks_ref, *refs):
    in_refs, (signals_ref, first_ref, second_ref) = refs[:7], refs[7:]
    chip, core = place()
    energies, lanes = in_refs[0].shape[1:]
    for j, pair in enumerate(blocks_of(in_refs, core)):
        for which, block in enumerate(pair):
            values = block()
            rows = energies_of(2 * (chip ^ j) + (core if which == 0 else 1 - core), energies)
            for part in range(2):
                signals_ref[rows, part * lanes : (part + 1) * lanes] = values[part]
    half = first_ref.shape[0]
    for i, ref in enumerate((first_ref, second_ref)):
        rows = slice(i * half, (i + 1) * half)
        ref[...] = (dot(signals_ref[rows, :lanes], picks_ref[3]) + dot(signals_ref[rows, lanes:], picks_ref[4])).astype(BF16)


def own_kernel(signals_ref, picks_ref, table_ref, near_ref, partner_ref):
    lanes = picks_ref.shape[-1]
    for part in range(2):
        cols = slice(part * lanes, (part + 1) * lanes)
        partner_ref[:, cols] = dot(signals_ref[:, cols], picks_ref[0]).astype(BF16)
    near_ref[...] = forward_sums(table_ref, signals_ref[...])


def exchange_kernel(flip_ref, near_ref, partner_ref, picks_ref, first_ref, first_far_ref, second_ref, second_far_ref, table_ref, *refs):
    (diagonal_ref, beside_ref, keep_ref, give_ref, own_ref), (held,) = refs[:5], refs[5:]
    chip, core = place()
    energies, lanes = own_ref.shape[1:]
    flip = flip_ref[0:1, :]
    far = jnp.concatenate(
        [
            jnp.where(flip == 1, first_ref[...], first_far_ref[...]),
            jnp.where(flip == 2, second_ref[...], second_far_ref[...]),
        ],
        axis=0,
    )
    partner = [
        (partner_ref[:, part * lanes : (part + 1) * lanes].astype(F32) + dot(far, picks_ref[1 + part])).astype(BF16)
        for part in range(2)
    ]
    held[...] = correlate(near_ref[...], forward_sums(table_ref, jnp.concatenate(partner, axis=-1)), table_ref)

    def block(device):
        rows = energies_of(device, energies)
        return [held[rows, part * lanes : (part + 1) * lanes] for part in range(2)]

    for j, ref in ((3, diagonal_ref), (2, beside_ref)):
        for which in range(2):
            for part, values in enumerate(block(2 * (chip ^ j) + which)):
                ref[which, part] = values
    for j, ref in ((1, keep_ref), (0, own_ref)):
        for part, values in enumerate(block(2 * (chip ^ j) + core)):
            ref[part] = values
        for part, values in enumerate(block(2 * (chip ^ j) + 1 - core)):
            give_ref[1 - j, part] = values


def join_kernel(*refs):
    in_refs, (lesser_ref, greater_ref) = refs[:7], refs[7:]
    chip, core = place()
    width = in_refs[0].shape[-1] // 2
    for j, (mine, other) in enumerate(blocks_of(in_refs, core)):
        mine, other = mine(), other()
        even = jnp.where(core == 0, mine, other)
        odd = jnp.where(core == 0, other, mine)
        cols = columns_of(chip ^ j, width)
        lesser_ref[:, :, cols] = jnp.concatenate([even[..., :width], odd[..., :width]], axis=-1)
        greater_ref[:, :, cols] = jnp.concatenate([even[..., width:], odd[..., width:]], axis=-1)


def four_chips(g_lesser, g_greater, send_rows, partner_slot):
    _, energies, group_rows = g_lesser.shape
    cap = send_rows.shape[-1]
    lanes = 4 * cap
    length = 8 * energies
    block = jax.ShapeDtypeStruct((2, energies, lanes), BF16)
    pair = jax.ShapeDtypeStruct((2, 2, energies, lanes), BF16)
    leaving = [pair, pair, block, pair, block]
    half = jax.ShapeDtypeStruct((length // 2, lanes), BF16)
    whole = jax.ShapeDtypeStruct((length, 2 * lanes), BF16)
    slots = partner_slot.reshape(4, lanes)
    table = jnp.asarray(fourier_tables(length))

    scratch = [
        pltpu.VMEM((4, 2, 2, energies, lanes), BF16),
        pltpu.VMEM(send_rows.shape[2:], jnp.int32),
        pltpu.VMEM(slots.shape, jnp.int32),
        pltpu.SemaphoreType.DMA((4, 2)),
        pltpu.SemaphoreType.DMA((2,)),
    ]
    tables = [jax.ShapeDtypeStruct((5, lanes, lanes), BF16), jax.ShapeDtypeStruct((8, lanes), jnp.int32)]
    *packed, picks, flip = call(
        split_kernel, leaving + tables, 2**24, send_rows, slots, g_lesser, g_greater, scratch=scratch, in_hbm=True
    )
    arrived = over_energy(*packed)
    signals, first, second = call(gather_kernel, [whole, half, half], 2**26, picks, *arrived)
    second_one, first_one = swap(second, "elem", 2), swap(first, "elem", 1)
    sums = jax.ShapeDtypeStruct((length, 2 * lanes), F32)
    near, partner = call(own_kernel, [sums, whole], 2**29, signals, picks, table)
    first_two = swap(call(relay_kernel, half, 0, flip, first_one, first), "elem", 2)
    second_two = swap(call(relay_kernel, half, 0, flip, second_one, second), "elem", 1)
    results = call(
        exchange_kernel,
        leaving,
        2**30,
        flip,
        near,
        partner,
        picks,
        first_one,
        first_two,
        second_one,
        second_two,
        table,
        scratch=[pltpu.VMEM((length, 2 * lanes), BF16)],
    )
    out = jax.ShapeDtypeStruct((2, energies, group_rows), BF16)
    return tuple(call(join_kernel, [out, out], 0, *over_energy(*results)))


def any_mesh(g_lesser, g_greater, send_rows, partner_slot):
    piece = lax.axis_index("energy")
    pieces = lax.axis_size("energy")
    _, energies, group_rows = g_lesser.shape
    groups, cap = send_rows.shape[2:]
    width = group_rows // pieces
    lanes = 2 * width
    length = pieces * energies
    packed_shape = jax.ShapeDtypeStruct((pieces, 2, energies, lanes), BF16)
    packed = call(pack_kernel, packed_shape, 0, g_lesser, g_greater)
    own = lax.all_to_all(packed, "energy", split_axis=0, concat_axis=0, tiled=True)
    rows = lax.dynamic_index_in_dim(send_rows[0], piece, 0, keepdims=False).reshape(-1)
    slots = lax.dynamic_slice_in_dim(partner_slot, piece * width, width, 0)
    pick = (jnp.arange(width, dtype=jnp.int32)[:, None] == rows[None, :]).astype(BF16)
    split = own.reshape(pieces, 2, energies, 2, width)
    outgoing = jnp.einsum("pceds,sm->mpced", split, pick, preferred_element_type=F32).astype(BF16)
    incoming = lax.all_to_all(outgoing, "elem", split_axis=0, concat_axis=0, tiled=True)
    table_width = groups * cap
    far = jnp.transpose(incoming, (1, 3, 2, 4, 0)).reshape(length, 4 * table_width)
    index = jnp.concatenate([slots + table_width, slots])
    index = jnp.stack([index, index + 2 * table_width])
    result = call(
        correlate_kernel,
        packed_shape,
        2 * length * length * lanes * 14,
        index,
        own,
        far,
        jnp.asarray(fourier_tables(length)),
    )
    back = lax.all_to_all(result, "energy", split_axis=0, concat_axis=0, tiled=True)
    out = jax.ShapeDtypeStruct((2, energies, group_rows), BF16)
    return tuple(call(unpack_kernel, [out, out], 0, back))


def shards(g_lesser, g_greater, send_rows, partner_slot):
    _, pieces, groups, cap = send_rows.shape
    fits = pieces == 8 and groups == 4 and cap == 32 and partner_slot.shape[0] == 512
    path = four_chips if fits else any_mesh
    return path(g_lesser, g_greater, send_rows, partner_slot)


def solution(mesh):
    in_specs = (
        P(None, "energy", "elem"),
        P(None, "energy", "elem"),
        P("elem", None, None, None),
        P("elem"),
    )
    out_specs = (P(None, "energy", "elem"), P(None, "energy", "elem"))
    return jax.shard_map(shards, mesh=mesh, in_specs=in_specs, out_specs=out_specs, check_vma=False)
```

```python
import functools
import math

import jax
import jax.numpy as jnp
import numpy as np
from jax import lax
from jax.experimental import pallas as pl
from jax.experimental.pallas import tpu as pltpu
from jax.sharding import PartitionSpec as P

BF16 = jnp.bfloat16
F32 = jnp.float32
VMEM_BYTES = 24 * 1024 * 1024


def fourier_tables(length):
    half = length // 2
    steps = np.arange(half)[:, None] * np.arange(length)[None, :] % length
    angle = steps * (2.0 * math.pi / length)
    sines = np.sin(angle)
    sines[0] = 1.0 - 2.0 * (np.arange(length) % 2)
    table = np.concatenate([np.cos(angle), sines], 0)

    def split(values):
        high = values.astype(np.float32).astype(jnp.bfloat16)
        low = (values - high.astype(np.float64)).astype(np.float32).astype(jnp.bfloat16)
        return np.stack([high, low])

    return np.concatenate([split(table), split(table.T)])


def pack_kernel(lesser_ref, greater_ref, out_ref):
    pieces, _, _, lanes = out_ref.shape
    width = lanes // 2
    for n in range(pieces):
        cols = slice(n * width, (n + 1) * width)
        out_ref[n] = jnp.concatenate([lesser_ref[:, :, cols], greater_ref[:, :, cols]], axis=-1)


def unpack_kernel(in_ref, lesser_ref, greater_ref):
    pieces, _, _, lanes = in_ref.shape
    width = lanes // 2
    per_tile = max(1, 128 // width)
    for first in range(0, pieces, per_tile):
        group = range(first, min(first + per_tile, pieces))
        cols = slice(first * width, (group[-1] + 1) * width)
        lesser_ref[:, :, cols] = jnp.concatenate([in_ref[n][:, :, :width] for n in group], axis=-1)
        greater_ref[:, :, cols] = jnp.concatenate([in_ref[n][:, :, width:] for n in group], axis=-1)


def one_hot(index_row, depth):
    rows = lax.broadcasted_iota(jnp.int32, (depth, index_row.shape[-1]), 0)
    return jnp.where(rows == index_row, 1.0, 0.0).astype(BF16)


def dot(a, b):
    return lax.dot_general(a, b, (((1,), (0,)), ((), ())), preferred_element_type=F32)


def rows_of(ref, part):
    blocks, _, energies, lanes = ref.shape
    return ref[:, part].reshape(blocks * energies, lanes)


def forward_sums(table_ref, signals):
    return dot(table_ref[0], signals) + dot(table_ref[1], signals)


def correlate(near, far, table_ref):
    half = near.shape[0] // 2
    length = near.shape[0]
    lanes = near.shape[1] // 2

    def parts(sums):
        return [sums[i * half : (i + 1) * half, j * lanes : (j + 1) * lanes] for i in range(2) for j in range(2)]

    a_re, a_im, b_re, b_im = parts(near)
    c_re, c_im, d_re, d_im = parts(far)
    first = lax.broadcasted_iota(jnp.int32, (half, lanes), 0) == 0
    ac_re, ac_im = a_re * c_re - a_im * c_im, a_re * c_im + a_im * c_re
    bd_re, bd_im = b_re * d_re - b_im * d_im, b_re * d_im + b_im * d_re
    u_re = jnp.where(first, 0.5 * ac_re, ac_re + bd_re)
    u_im = jnp.where(first, 0.5 * ac_im, ac_im + bd_im)
    v_re = jnp.where(first, 0.5 * bd_re, b_re * c_re - b_im * c_im - (a_re * d_re - a_im * d_im))
    v_im = jnp.where(first, 0.5 * bd_im, b_re * c_im + b_im * c_re - (a_re * d_im + a_im * d_re))
    top = jnp.concatenate([u_im, -u_re], axis=-1)
    bottom = jnp.concatenate([v_im, -v_re], axis=-1)
    products = jnp.concatenate([top, bottom], axis=0)
    high = products.astype(BF16)
    low = (products - high.astype(F32)).astype(BF16)
    back = dot(table_ref[2], high) + (dot(table_ref[2], low) + dot(table_ref[3], high))
    return (back * (2.0 / (length * math.sqrt(length)))).astype(BF16)


def correlate_kernel(index_ref, own_ref, far_ref, table_ref, out_ref):
    blocks, _, energies, lanes = own_ref.shape
    far = far_ref[...]
    own, partner = [], []
    for part in range(2):
        pick_far = one_hot(index_ref[part : part + 1, :], far.shape[-1])
        own.append(rows_of(own_ref, part))
        partner.append(dot(far, pick_far).astype(BF16))
    near = forward_sums(table_ref, jnp.concatenate(own, axis=-1))
    result = correlate(near, forward_sums(table_ref, jnp.concatenate(partner, axis=-1)), table_ref)
    for part in range(2):
        out_ref[:, part] = result[:, part * lanes : (part + 1) * lanes].reshape(blocks, energies, lanes)


def call(kernel, out_shape, flops, *args, scratch=(), in_hbm=()):
    outs = out_shape if isinstance(out_shape, (list, tuple)) else [out_shape]
    moved = sum(math.prod(v.shape) * v.dtype.itemsize for v in [*args, *outs])
    spaces = [pltpu.HBM if i in in_hbm else pltpu.VMEM for i in range(len(args))]
    args = [pltpu.with_memory_space_constraint(v, pltpu.HBM) if i in in_hbm else v for i, v in enumerate(args)]
    return pl.pallas_call(
        kernel,
        out_shape=out_shape,
        in_specs=[pl.BlockSpec(memory_space=space) for space in spaces],
        scratch_shapes=list(scratch),
        compiler_params=pltpu.CompilerParams(vmem_limit_bytes=VMEM_BYTES),
        cost_estimate=pl.CostEstimate(flops=flops, bytes_accessed=moved, transcendentals=0),
    )(*args)


def place():
    me = lax.axis_index("energy")
    return me // 2, me % 2


def columns_of(chip, width):
    return pl.ds(pl.multiple_of(chip * 2 * width, 2 * width), 2 * width)


def split_kernel(lists_ref, slots_ref, lesser_ref, greater_ref, *refs):
    (diagonal_ref, keep_ref, give_ref, picks_ref, flip_ref) = refs[:5]
    held, lists, slots, sems, index_sems = refs[5:]
    chip, core = place()
    index_copies = [
        pltpu.make_async_copy(lists_ref.at[0, 2 * chip + core], lists, index_sems.at[0]),
        pltpu.make_async_copy(slots_ref, slots, index_sems.at[1]),
    ]
    for copy in index_copies:
        copy.start()
    width = keep_ref.shape[-1] // 2
    copies = [
        [
            pltpu.make_async_copy(ref.at[:, :, columns_of(chip ^ j, width)], held.at[j, i], sems.at[j, i])
            for i, ref in enumerate((lesser_ref, greater_ref))
        ]
        for j in range(4)
    ]
    for j in (3, 2, 1, 0):
        for copy in copies[j]:
            copy.start()
    for copy in index_copies:
        copy.wait()
    index_tables(lists[...], slots[pl.ds(chip, 1), :], picks_ref, flip_ref)
    for j in (3, 2, 1, 0):
        for copy in copies[j]:
            copy.wait()
        lesser, greater = held[j, 0], held[j, 1]
        zero = jnp.concatenate([lesser[..., :width], greater[..., :width]], axis=-1)
        one = jnp.concatenate([lesser[..., width:], greater[..., width:]], axis=-1)
        if j == 3:
            diagonal_ref[0], diagonal_ref[1] = zero, one
        else:
            keep_ref[j] = jnp.where(core == 0, zero, one)
            give_ref[j] = jnp.where(core == 0, one, zero)


def swap(values, axis, bit):
    return lax.ppermute(values, axis, [(i, i ^ bit) for i in range(lax.axis_size(axis))])


def over_elem(values, bits):
    groups = lax.axis_size("elem")
    pairs = [(n * groups + i, n * groups + (i ^ bits[n % 2])) for n in range(lax.axis_size("energy")) for i in range(groups)]
    return lax.ppermute(values, ("energy", "elem"), pairs)


def over_energy(diagonal, keep, give):
    diagonal = swap(diagonal, "energy", 6)
    got = swap(give, "energy", 1)
    beside = swap(jnp.stack([keep[2], got[2]]), "energy", 4)
    across = swap(jnp.stack([keep[1], got[1]]), "energy", 2)
    diagonal, beside = lax.optimization_barrier((diagonal, beside))
    return keep, got, diagonal, swap(diagonal, "energy", 1), beside, across


def blocks_of(refs, core):
    keep_ref, got_ref, diagonal_ref, diagonal_other_ref, beside_ref, across_ref = refs
    return [
        (lambda: keep_ref[0], lambda: got_ref[0]),
        (lambda: across_ref[0], lambda: across_ref[1]),
        (lambda: beside_ref[0], lambda: beside_ref[1]),
        (lambda: diagonal_ref[core], lambda: diagonal_other_ref[core]),
    ]


def lane_row(lanes):
    return lax.broadcasted_iota(jnp.int32, (1, lanes), 1)


def energies_of(device, energies):
    return pl.ds(pl.multiple_of(device * energies, energies), energies)


def repeat(values, index_row):
    return dot(values.astype(F32).astype(BF16), one_hot(index_row, values.shape[-1])).astype(jnp.int32)


def relay_kernel(flip_ref, first_ref, own_ref, _, out_ref):
    out_ref[...] = jnp.where(flip_ref[0:1, :] == 3, first_ref[...], own_ref[...])


def index_tables(lists, slots, picks_ref, flip_ref):
    _, core = place()
    group = lax.axis_index("elem")
    lanes = picks_ref.shape[-1]
    width, cap = lanes // 2, lanes // 4
    lane = lane_row(lanes)
    lists = repeat(lists, lane % cap)
    ids = lax.broadcasted_iota(jnp.int32, lists.shape, 0)
    greater = jnp.where(lane // cap % 2 == 1, width, 0)
    near_rows = jnp.sum(jnp.where(ids == group, lists, 0), axis=0, keepdims=True) + greater
    far_rows = jnp.sum(jnp.where(ids == group, 0, lists), axis=0, keepdims=True) + greater
    filled = jnp.max(lists, axis=1, keepdims=True) > 0
    flip = jnp.sum(jnp.where(filled, ids ^ group, 0), axis=0, keepdims=True)
    flip_ref[...] = jnp.broadcast_to(flip[:, :1], flip_ref.shape)
    slots = repeat(slots, core * width + lane % width)
    source = slots // cap
    spot = slots - source * cap + jnp.where(lane < width, cap, 0)
    near = one_hot(jnp.where(lane < 2 * cap, near_rows, -1), lanes)
    picks_ref[0] = dot(near, one_hot(jnp.where(source == group, spot, -1), lanes)).astype(BF16)
    for part in range(2):
        picks_ref[1 + part] = one_hot(jnp.where(source == group, -1, spot + 2 * cap * part), lanes)
        picks_ref[3 + part] = one_hot(jnp.where(lane // (2 * cap) == part, far_rows, -1), lanes)


def gather_kernel(picks_ref, *refs):
    in_refs, (signals_ref, sent_ref) = refs[:6], refs[6:]
    chip, core = place()
    energies, lanes = in_refs[0].shape[2:]
    for j, pair in enumerate(blocks_of(in_refs, core)):
        for which, block in enumerate(pair):
            values = block()
            rows = energies_of(2 * (chip ^ j) + (core if which == 0 else 1 - core), energies)
            for part in range(2):
                signals_ref[rows, part * lanes : (part + 1) * lanes] = values[part]
    sent_ref[...] = (dot(signals_ref[:, :lanes], picks_ref[3]) + dot(signals_ref[:, lanes:], picks_ref[4])).astype(BF16)


def own_kernel(signals_ref, picks_ref, table_ref, near_ref, partner_ref, held_ref, sems):
    lanes = picks_ref.shape[-1]
    steps = sems.shape[0] // 4
    height = table_ref.shape[1] // steps
    copies = []
    for i in range(4 * steps):
        rows = pl.ds(i % steps * height, height)
        copies.append(pltpu.make_async_copy(table_ref.at[i // steps, rows], held_ref.at[i // steps, rows], sems.at[i]))
    for copy in copies:
        copy.start()
    for part in range(2):
        cols = slice(part * lanes, (part + 1) * lanes)
        partner_ref[:, cols] = dot(signals_ref[:, cols], picks_ref[0]).astype(BF16)
    for copy in copies:
        copy.wait()
    near_ref[...] = forward_sums(held_ref, signals_ref[...])


def exchange_kernel(flip_ref, near_ref, partner_ref, picks_ref, first_ref, second_ref, table_ref, *refs):
    (diagonal_ref, keep_ref, give_ref), (held,) = refs[:3], refs[3:]
    chip, core = place()
    energies, lanes = keep_ref.shape[2:]
    far = jnp.where(flip_ref[0:1, :] == 1 + core, first_ref[...], second_ref[...])
    partner = [
        (partner_ref[:, part * lanes : (part + 1) * lanes].astype(F32) + dot(far, picks_ref[1 + part])).astype(BF16)
        for part in range(2)
    ]
    held[...] = correlate(near_ref[...], forward_sums(table_ref, jnp.concatenate(partner, axis=-1)), table_ref)

    def block(j, core):
        rows = energies_of(2 * (chip ^ j) + core, energies)
        return [held[rows, part * lanes : (part + 1) * lanes] for part in range(2)]

    for which in range(2):
        diagonal_ref[which, 0], diagonal_ref[which, 1] = block(3, which)
    for j in range(3):
        keep_ref[j, 0], keep_ref[j, 1] = block(j, core)
        give_ref[j, 0], give_ref[j, 1] = block(j, 1 - core)


def join_kernel(*refs):
    in_refs, (lesser_ref, greater_ref) = refs[:6], refs[6:]
    chip, core = place()
    width = in_refs[0].shape[-1] // 2
    for j, (mine, other) in enumerate(blocks_of(in_refs, core)):
        mine, other = mine(), other()
        even = jnp.where(core == 0, mine, other)
        odd = jnp.where(core == 0, other, mine)
        cols = columns_of(chip ^ j, width)
        lesser_ref[:, :, cols] = jnp.concatenate([even[..., :width], odd[..., :width]], axis=-1)
        greater_ref[:, :, cols] = jnp.concatenate([even[..., width:], odd[..., width:]], axis=-1)


def four_chips(g_lesser, g_greater, send_rows, partner_slot):
    _, energies, group_rows = g_lesser.shape
    cap = send_rows.shape[-1]
    lanes = 4 * cap
    length = 8 * energies
    pair = jax.ShapeDtypeStruct((2, 2, energies, lanes), BF16)
    three = jax.ShapeDtypeStruct((3, 2, energies, lanes), BF16)
    leaving = [pair, three, three]
    column = jax.ShapeDtypeStruct((length, lanes), BF16)
    whole = jax.ShapeDtypeStruct((length, 2 * lanes), BF16)
    slots = partner_slot.reshape(4, lanes)
    table = jnp.asarray(fourier_tables(length))

    scratch = [
        pltpu.VMEM((4, 2, 2, energies, lanes), BF16),
        pltpu.VMEM(send_rows.shape[2:], jnp.int32),
        pltpu.VMEM(slots.shape, jnp.int32),
        pltpu.SemaphoreType.DMA((4, 2)),
        pltpu.SemaphoreType.DMA((2,)),
    ]
    tables = [jax.ShapeDtypeStruct((5, lanes, lanes), BF16), jax.ShapeDtypeStruct((8, lanes), jnp.int32)]
    *packed, picks, flip = call(
        split_kernel, leaving + tables, 2**24, send_rows, slots, g_lesser, g_greater, scratch=scratch, in_hbm=(0, 1, 2, 3)
    )
    signals, sent = call(gather_kernel, [whole, column], 2**26, picks, *over_energy(*packed))
    first = over_elem(sent, (1, 2))
    near, partner, held = call(
        own_kernel,
        [jax.ShapeDtypeStruct(whole.shape, F32), whole, jax.ShapeDtypeStruct(table.shape, BF16)],
        2**29,
        signals,
        picks,
        table,
        scratch=[pltpu.SemaphoreType.DMA((16,))],
        in_hbm=(2,),
    )
    second = over_elem(call(relay_kernel, column, 0, flip, first, sent, partner), (2, 1))
    results = call(
        exchange_kernel,
        leaving,
        2**30,
        flip,
        near,
        partner,
        picks,
        first,
        second,
        held,
        scratch=[pltpu.VMEM(whole.shape, BF16)],
    )
    out = jax.ShapeDtypeStruct((2, energies, group_rows), BF16)
    return tuple(call(join_kernel, [out, out], 0, *over_energy(*results)))


def any_mesh(g_lesser, g_greater, send_rows, partner_slot):
    piece = lax.axis_index("energy")
    pieces = lax.axis_size("energy")
    _, energies, group_rows = g_lesser.shape
    groups, cap = send_rows.shape[2:]
    width = group_rows // pieces
    lanes = 2 * width
    length = pieces * energies
    packed_shape = jax.ShapeDtypeStruct((pieces, 2, energies, lanes), BF16)
    packed = call(pack_kernel, packed_shape, 0, g_lesser, g_greater)
    own = lax.all_to_all(packed, "energy", split_axis=0, concat_axis=0, tiled=True)
    rows = lax.dynamic_index_in_dim(send_rows[0], piece, 0, keepdims=False).reshape(-1)
    slots = lax.dynamic_slice_in_dim(partner_slot, piece * width, width, 0)
    pick = (jnp.arange(width, dtype=jnp.int32)[:, None] == rows[None, :]).astype(BF16)
    split = own.reshape(pieces, 2, energies, 2, width)
    outgoing = jnp.einsum("pceds,sm->mpced", split, pick, preferred_element_type=F32).astype(BF16)
    incoming = lax.all_to_all(outgoing, "elem", split_axis=0, concat_axis=0, tiled=True)
    table_width = groups * cap
    far = jnp.transpose(incoming, (1, 3, 2, 4, 0)).reshape(length, 4 * table_width)
    index = jnp.concatenate([slots + table_width, slots])
    index = jnp.stack([index, index + 2 * table_width])
    result = call(
        correlate_kernel,
        packed_shape,
        2 * length * length * lanes * 14,
        index,
        own,
        far,
        jnp.asarray(fourier_tables(length)),
    )
    back = lax.all_to_all(result, "energy", split_axis=0, concat_axis=0, tiled=True)
    out = jax.ShapeDtypeStruct((2, energies, group_rows), BF16)
    return tuple(call(unpack_kernel, [out, out], 0, back))


def shards(g_lesser, g_greater, send_rows, partner_slot):
    _, pieces, groups, cap = send_rows.shape
    fits = pieces == 8 and groups == 4 and cap == 32 and partner_slot.shape[0] == 512
    path = four_chips if fits else any_mesh
    return path(g_lesser, g_greater, send_rows, partner_slot)


def solution(mesh):
    in_specs = (
        P(None, "energy", "elem"),
        P(None, "energy", "elem"),
        P("elem", None, None, None),
        P("elem"),
    )
    out_specs = (P(None, "energy", "elem"), P(None, "energy", "elem"))
    return jax.shard_map(shards, mesh=mesh, in_specs=in_specs, out_specs=out_specs, check_vma=False)
```

```python
import functools
import math

import jax
import jax.numpy as jnp
import numpy as np
from jax import lax
from jax.experimental import pallas as pl
from jax.experimental.pallas import tpu as pltpu
from jax.sharding import PartitionSpec as P

BF16 = jnp.bfloat16
F32 = jnp.float32
VMEM_BYTES = 24 * 1024 * 1024


def fourier_tables(length):
    half = length // 2
    steps = np.arange(half)[:, None] * np.arange(length)[None, :] % length
    angle = steps * (2.0 * math.pi / length)
    sines = np.sin(angle)
    sines[0] = 1.0 - 2.0 * (np.arange(length) % 2)
    table = np.concatenate([np.cos(angle), sines], 0)

    def split(values):
        high = values.astype(np.float32).astype(jnp.bfloat16)
        low = (values - high.astype(np.float64)).astype(np.float32).astype(jnp.bfloat16)
        return np.stack([high, low])

    return np.concatenate([split(table), split(table.T)])


def pack_kernel(lesser_ref, greater_ref, out_ref):
    pieces, _, _, lanes = out_ref.shape
    width = lanes // 2
    for n in range(pieces):
        cols = slice(n * width, (n + 1) * width)
        out_ref[n] = jnp.concatenate([lesser_ref[:, :, cols], greater_ref[:, :, cols]], axis=-1)


def unpack_kernel(in_ref, lesser_ref, greater_ref):
    pieces, _, _, lanes = in_ref.shape
    width = lanes // 2
    per_tile = max(1, 128 // width)
    for first in range(0, pieces, per_tile):
        group = range(first, min(first + per_tile, pieces))
        cols = slice(first * width, (group[-1] + 1) * width)
        lesser_ref[:, :, cols] = jnp.concatenate([in_ref[n][:, :, :width] for n in group], axis=-1)
        greater_ref[:, :, cols] = jnp.concatenate([in_ref[n][:, :, width:] for n in group], axis=-1)


def one_hot(index_row, depth):
    rows = lax.broadcasted_iota(jnp.int32, (depth, index_row.shape[-1]), 0)
    return jnp.where(rows == index_row, 1.0, 0.0).astype(BF16)


def dot(a, b):
    return lax.dot_general(a, b, (((1,), (0,)), ((), ())), preferred_element_type=F32)


def rows_of(ref, part):
    blocks, _, energies, lanes = ref.shape
    return ref[:, part].reshape(blocks * energies, lanes)


def forward_sums(table_ref, signals):
    return dot(table_ref[0], signals) + dot(table_ref[1], signals)


def correlate(near, far, table_ref):
    half = near.shape[0] // 2
    length = near.shape[0]
    lanes = near.shape[1] // 2

    def parts(sums):
        return [sums[i * half : (i + 1) * half, j * lanes : (j + 1) * lanes] for i in range(2) for j in range(2)]

    a_re, a_im, b_re, b_im = parts(near)
    c_re, c_im, d_re, d_im = parts(far)
    first = lax.broadcasted_iota(jnp.int32, (half, lanes), 0) == 0
    ac_re, ac_im = a_re * c_re - a_im * c_im, a_re * c_im + a_im * c_re
    bd_re, bd_im = b_re * d_re - b_im * d_im, b_re * d_im + b_im * d_re
    u_re = jnp.where(first, 0.5 * ac_re, ac_re + bd_re)
    u_im = jnp.where(first, 0.5 * ac_im, ac_im + bd_im)
    v_re = jnp.where(first, 0.5 * bd_re, b_re * c_re - b_im * c_im - (a_re * d_re - a_im * d_im))
    v_im = jnp.where(first, 0.5 * bd_im, b_re * c_im + b_im * c_re - (a_re * d_im + a_im * d_re))
    top = jnp.concatenate([u_im, -u_re], axis=-1)
    bottom = jnp.concatenate([v_im, -v_re], axis=-1)
    products = jnp.concatenate([top, bottom], axis=0)
    high = products.astype(BF16)
    low = (products - high.astype(F32)).astype(BF16)
    back = dot(table_ref[2], high) + (dot(table_ref[2], low) + dot(table_ref[3], high))
    return (back * (2.0 / (length * math.sqrt(length)))).astype(BF16)


def correlate_kernel(index_ref, own_ref, far_ref, table_ref, out_ref):
    blocks, _, energies, lanes = own_ref.shape
    far = far_ref[...]
    own, partner = [], []
    for part in range(2):
        pick_far = one_hot(index_ref[part : part + 1, :], far.shape[-1])
        own.append(rows_of(own_ref, part))
        partner.append(dot(far, pick_far).astype(BF16))
    near = forward_sums(table_ref, jnp.concatenate(own, axis=-1))
    result = correlate(near, forward_sums(table_ref, jnp.concatenate(partner, axis=-1)), table_ref)
    for part in range(2):
        out_ref[:, part] = result[:, part * lanes : (part + 1) * lanes].reshape(blocks, energies, lanes)


def call(kernel, out_shape, flops, *args, scratch=(), in_hbm=(), out_smem=()):
    many = isinstance(out_shape, (list, tuple))
    outs = list(out_shape) if many else [out_shape]
    moved = sum(math.prod(v.shape) * v.dtype.itemsize for v in [*args, *outs])


    def specs(values, elsewhere, space):
        return [pl.BlockSpec(memory_space=space if i in elsewhere else pltpu.VMEM) for i in range(len(values))]

    out_specs = specs(outs, out_smem, pltpu.SMEM)
    args = [pltpu.with_memory_space_constraint(v, pltpu.HBM) if i in in_hbm else v for i, v in enumerate(args)]
    return pl.pallas_call(
        kernel,
        out_shape=out_shape,
        in_specs=specs(args, in_hbm, pltpu.HBM),
        out_specs=out_specs if many else out_specs[0],
        scratch_shapes=list(scratch),
        compiler_params=pltpu.CompilerParams(vmem_limit_bytes=VMEM_BYTES),
        cost_estimate=pl.CostEstimate(flops=flops, bytes_accessed=moved, transcendentals=0),
    )(*args)


def place():
    me = lax.axis_index("energy")
    return me // 2, me % 2


def columns_of(chip, width):
    return pl.ds(pl.multiple_of(chip * 2 * width, 2 * width), 2 * width)


def distances(lists_ref, plan_ref):
    pieces, groups, _ = lists_ref.shape
    group = lax.axis_index("elem")
    distance = []
    for n in range(pieces):
        found = jnp.int32(0)
        for i in range(groups):
            filled = lists_ref[n, i, 0] + lists_ref[n, i, 1] > 0
            found = found + jnp.where(jnp.logical_and(filled, group != i), group ^ i, 0)
        distance.append(found)
    near = [jnp.where(d == 1, 1, 0) for d in distance]
    middle = [jnp.where(d == 2, 1, 0) for d in distance]
    count_near, count_middle = sum(near), sum(middle)
    seen_near, seen_middle, seen_far = jnp.int32(0), count_near, count_near + count_middle
    for n in range(pieces):
        far = 1 - near[n] - middle[n]
        rank = near[n] * seen_near + middle[n] * seen_middle + far * seen_far
        seen_near, seen_middle, seen_far = seen_near + near[n], seen_middle + middle[n], seen_far + far
        line = 2 * (rank % (pieces // 2)) + rank // (pieces // 2)
        plan_ref[line] = jnp.int32(n)
        plan_ref[pieces + n] = line
    plan_ref[2 * pieces] = count_near * (pieces + 1) - count_near * (count_near - 1) // 2 + count_middle


def counts_of(pieces):
    return [(near, middle) for near in range(pieces + 1) for middle in range(pieces + 1 - near)]


def over_elem(number, values, beside, *args):
    pieces, groups = lax.axis_size("energy"), lax.axis_size("elem")

    def branch(near, middle):
        ranked = [1] * near + [2] * middle + [3] * (pieces - near - middle)
        by_line = [ranked[n // 2 + pieces // 2 * (n % 2)] for n in range(pieces)]
        pairs = [(n * groups + i, n * groups + (i ^ by_line[n])) for n in range(pieces) for i in range(groups)]
        return lambda sent, *args: (lax.ppermute(sent, ("energy", "elem"), pairs), *beside(*args))

    return lax.switch(number, [branch(*counts) for counts in counts_of(pieces)], values, *args)


def split_kernel(lists_ref, slots_ref, lesser_ref, greater_ref, *refs):
    (diagonal_ref, keep_ref, give_ref, picks_ref, number_ref, lines_ref) = refs[:6]
    lesser, greater, lists, slots, packed, scalars, plan_ref, sems = refs[6:]
    chip, core = place()
    pairs = [(lists_ref, scalars), (lists_ref, lists), (slots_ref, slots), (lesser_ref, lesser), (greater_ref, greater)]
    copies = [pltpu.make_async_copy(source, target, sems.at[i]) for i, (source, target) in enumerate(pairs)]
    for copy in copies:
        copy.start()
    for copy in copies[:3]:
        copy.wait()
    distances(scalars, plan_ref)
    pieces = packed.shape[0]
    number_ref[0] = plan_ref[2 * pieces]
    lines_ref[...] = jnp.full(lines_ref.shape, sum(plan_ref[pieces + n] * 8**n for n in range(pieces)), jnp.int32)
    piece = plan_ref[2 * chip + core]
    index_tables(lists[piece], slots[pl.ds(piece // 2, 1), :], piece % 2, picks_ref)
    for copy in copies[3:]:
        copy.wait()
    width = packed.shape[-1] // 2
    for n in range(pieces):
        cols = slice(n * width, (n + 1) * width)
        packed[n] = jnp.concatenate([lesser[:, :, cols], greater[:, :, cols]], axis=-1)
    for which in range(2):
        diagonal_ref[which] = packed[plan_ref[2 * (chip ^ 3) + which]]
    for j in range(3):
        keep_ref[j] = packed[plan_ref[2 * (chip ^ j) + core]]
        give_ref[j] = packed[plan_ref[2 * (chip ^ j) + 1 - core]]


def swap(values, axis, bit):
    return lax.ppermute(values, axis, [(i, i ^ bit) for i in range(lax.axis_size(axis))])


def over_energy(diagonal, keep, give):
    diagonal = swap(diagonal, "energy", 6)
    got = swap(give, "energy", 1)
    beside = swap(jnp.stack([keep[2], got[2]]), "energy", 4)
    across = swap(jnp.stack([keep[1], got[1]]), "energy", 2)
    diagonal, beside = lax.optimization_barrier((diagonal, beside))
    return keep, got, diagonal, swap(diagonal, "energy", 1), beside, across


def blocks_of(refs, core):
    keep_ref, got_ref, diagonal_ref, diagonal_other_ref, beside_ref, across_ref = refs
    return [
        (lambda: keep_ref[0], lambda: got_ref[0]),
        (lambda: across_ref[0], lambda: across_ref[1]),
        (lambda: beside_ref[0], lambda: beside_ref[1]),
        (lambda: diagonal_ref[core], lambda: diagonal_other_ref[core]),
    ]


def lane_row(lanes):
    return lax.broadcasted_iota(jnp.int32, (1, lanes), 1)


def energies_of(device, energies):
    return pl.ds(pl.multiple_of(device * energies, energies), energies)


def repeat(values, index_row):
    return dot(values.astype(F32).astype(BF16), one_hot(index_row, values.shape[-1])).astype(jnp.int32)


def index_tables(lists, slots, odd, picks_ref):
    group = lax.axis_index("elem")
    lanes = picks_ref.shape[-1]
    width, cap = lanes // 2, lanes // 4
    lane = lane_row(lanes)
    lists = repeat(lists, lane % cap)
    ids = lax.broadcasted_iota(jnp.int32, lists.shape, 0)
    greater = jnp.where(lane // cap % 2 == 1, width, 0)
    near_rows = jnp.sum(jnp.where(ids == group, lists, 0), axis=0, keepdims=True) + greater
    far_rows = jnp.sum(jnp.where(ids == group, 0, lists), axis=0, keepdims=True) + greater
    slots = repeat(slots, odd * width + lane % width)
    source = slots // cap
    spot = slots - source * cap + jnp.where(lane < width, cap, 0)
    near = one_hot(jnp.where(lane < 2 * cap, near_rows, -1), lanes)
    picks_ref[0] = dot(near, one_hot(jnp.where(source == group, spot, -1), lanes)).astype(BF16)
    for part in range(2):
        picks_ref[1 + part] = one_hot(jnp.where(source == group, -1, spot + 2 * cap * part), lanes)
        picks_ref[3 + part] = one_hot(jnp.where(lane // (2 * cap) == part, far_rows, -1), lanes)


def gather_kernel(picks_ref, *refs):
    in_refs, (signals_ref, sent_ref) = refs[:6], refs[6:]
    chip, core = place()
    energies, lanes = in_refs[0].shape[2:]
    for j, pair in enumerate(blocks_of(in_refs, core)):
        for which, block in enumerate(pair):
            values = block()
            rows = energies_of(2 * (chip ^ j) + (core if which == 0 else 1 - core), energies)
            for part in range(2):
                signals_ref[rows, part * lanes : (part + 1) * lanes] = values[part]
    sent_ref[...] = (dot(signals_ref[:, :lanes], picks_ref[3]) + dot(signals_ref[:, lanes:], picks_ref[4])).astype(BF16)


def own_kernel(signals_ref, picks_ref, table_ref, sums_ref, partner_ref, held_ref, sems):
    lanes = picks_ref.shape[-1]
    steps = sems.shape[0] // 4
    height = table_ref.shape[1] // steps
    copies = []
    for i in range(4 * steps):
        rows = pl.ds(i % steps * height, height)
        copies.append(pltpu.make_async_copy(table_ref.at[i // steps, rows], held_ref.at[i // steps, rows], sems.at[i]))
    for copy in copies:
        copy.start()
    for part in range(2):
        cols = slice(part * lanes, (part + 1) * lanes)
        partner_ref[:, cols] = dot(signals_ref[:, cols], picks_ref[0]).astype(BF16)
    for copy in copies:
        copy.wait()
    sums_ref[...] = forward_sums(held_ref, signals_ref[...])


def exchange_kernel(sums_ref, partner_ref, picks_ref, far_ref, table_ref, *refs):
    (diagonal_ref, keep_ref, give_ref), (held,) = refs[:3], refs[3:]
    chip, core = place()
    energies, lanes = keep_ref.shape[2:]
    far = far_ref[...]
    partner = [
        (partner_ref[:, part * lanes : (part + 1) * lanes].astype(F32) + dot(far, picks_ref[1 + part])).astype(BF16)
        for part in range(2)
    ]
    held[...] = correlate(sums_ref[...], forward_sums(table_ref, jnp.concatenate(partner, axis=-1)), table_ref)

    def block(j, core):
        rows = energies_of(2 * (chip ^ j) + core, energies)
        return [held[rows, part * lanes : (part + 1) * lanes] for part in range(2)]

    for which in range(2):
        diagonal_ref[which, 0], diagonal_ref[which, 1] = block(3, which)
    for j in range(3):
        keep_ref[j, 0], keep_ref[j, 1] = block(j, core)
        give_ref[j, 0], give_ref[j, 1] = block(j, 1 - core)


def join_kernel(lines_ref, *refs):
    in_refs, (lesser_ref, greater_ref, held) = refs[:6], refs[6:]
    chip, core = place()
    width = held.shape[-1] // 2
    for j, (mine, other) in enumerate(blocks_of(in_refs, core)):
        held[2 * (chip ^ j) + core] = mine()
        held[2 * (chip ^ j) + 1 - core] = other()
    lines = jnp.max(lines_ref[...])
    for n in range(0, held.shape[0], 2):
        even, odd = held[lines // 8**n % 8], held[lines // 8 ** (n + 1) % 8]
        cols = slice(n * width, (n + 2) * width)
        lesser_ref[:, :, cols] = jnp.concatenate([even[..., :width], odd[..., :width]], axis=-1)
        greater_ref[:, :, cols] = jnp.concatenate([even[..., width:], odd[..., width:]], axis=-1)


def four_chips(g_lesser, g_greater, send_rows, partner_slot):
    _, energies, group_rows = g_lesser.shape
    cap = send_rows.shape[-1]
    lanes = 4 * cap
    length = 8 * energies
    pair = jax.ShapeDtypeStruct((2, 2, energies, lanes), BF16)
    three = jax.ShapeDtypeStruct((3, 2, energies, lanes), BF16)
    leaving = [pair, three, three]
    column = jax.ShapeDtypeStruct((length, lanes), BF16)
    whole = jax.ShapeDtypeStruct((length, 2 * lanes), BF16)
    slots = partner_slot.reshape(4, lanes)
    table = jnp.asarray(fourier_tables(length))

    scratch = [
        pltpu.VMEM(g_lesser.shape, BF16),
        pltpu.VMEM(g_lesser.shape, BF16),
        pltpu.VMEM(send_rows.shape[1:], jnp.int32),
        pltpu.VMEM(slots.shape, jnp.int32),
        pltpu.VMEM((8, 2, energies, lanes), BF16),
        pltpu.SMEM(send_rows.shape[1:], jnp.int32),
        pltpu.SMEM((17,), jnp.int32),
        pltpu.SemaphoreType.DMA((5,)),
    ]
    more = [
        jax.ShapeDtypeStruct((5, lanes, lanes), BF16),
        jax.ShapeDtypeStruct((1,), jnp.int32),
        jax.ShapeDtypeStruct((8, lanes), jnp.int32),
    ]
    *packed, picks, number, lines = call(
        split_kernel,
        leaving + more,
        2**24,
        send_rows[0],
        slots,
        g_lesser,
        g_greater,
        scratch=scratch,
        in_hbm=(0, 1, 2, 3),
        out_smem=(4,),
    )

    signals, sent = call(gather_kernel, [whole, column], 2**26, picks, *over_energy(*packed))

    def own(*args):
        shapes = [jax.ShapeDtypeStruct(whole.shape, F32), whole, jax.ShapeDtypeStruct(table.shape, BF16)]
        return call(own_kernel, shapes, 2**29, *args, scratch=[pltpu.SemaphoreType.DMA((16,))], in_hbm=(2,))

    far, sums, partner, held = over_elem(number[0], sent, own, signals, picks, table)
    results = call(
        exchange_kernel, leaving, 2**30, sums, partner, picks, far, held, scratch=[pltpu.VMEM(whole.shape, BF16)]
    )
    out = jax.ShapeDtypeStruct((2, energies, group_rows), BF16)
    scratch = [pltpu.VMEM((8, 2, energies, lanes), BF16)]
    return tuple(call(join_kernel, [out, out], 0, lines, *over_energy(*results), scratch=scratch))


def any_mesh(g_lesser, g_greater, send_rows, partner_slot):
    piece = lax.axis_index("energy")
    pieces = lax.axis_size("energy")
    _, energies, group_rows = g_lesser.shape
    groups, cap = send_rows.shape[2:]
    width = group_rows // pieces
    lanes = 2 * width
    length = pieces * energies
    packed_shape = jax.ShapeDtypeStruct((pieces, 2, energies, lanes), BF16)
    packed = call(pack_kernel, packed_shape, 0, g_lesser, g_greater)
    own = lax.all_to_all(packed, "energy", split_axis=0, concat_axis=0, tiled=True)
    rows = lax.dynamic_index_in_dim(send_rows[0], piece, 0, keepdims=False).reshape(-1)
    slots = lax.dynamic_slice_in_dim(partner_slot, piece * width, width, 0)
    pick = (jnp.arange(width, dtype=jnp.int32)[:, None] == rows[None, :]).astype(BF16)
    split = own.reshape(pieces, 2, energies, 2, width)
    outgoing = jnp.einsum("pceds,sm->mpced", split, pick, preferred_element_type=F32).astype(BF16)
    incoming = lax.all_to_all(outgoing, "elem", split_axis=0, concat_axis=0, tiled=True)
    table_width = groups * cap
    far = jnp.transpose(incoming, (1, 3, 2, 4, 0)).reshape(length, 4 * table_width)
    index = jnp.concatenate([slots + table_width, slots])
    index = jnp.stack([index, index + 2 * table_width])
    result = call(
        correlate_kernel,
        packed_shape,
        2 * length * length * lanes * 14,
        index,
        own,
        far,
        jnp.asarray(fourier_tables(length)),
    )
    back = lax.all_to_all(result, "energy", split_axis=0, concat_axis=0, tiled=True)
    out = jax.ShapeDtypeStruct((2, energies, group_rows), BF16)
    return tuple(call(unpack_kernel, [out, out], 0, back))


def shards(g_lesser, g_greater, send_rows, partner_slot):
    _, pieces, groups, cap = send_rows.shape
    fits = pieces == 8 and groups == 4 and cap == 32 and partner_slot.shape[0] == 512
    path = four_chips if fits else any_mesh
    return path(g_lesser, g_greater, send_rows, partner_slot)


def solution(mesh):
    in_specs = (
        P(None, "energy", "elem"),
        P(None, "energy", "elem"),
        P("elem", None, None, None),
        P("elem"),
    )
    out_specs = (P(None, "energy", "elem"), P(None, "energy", "elem"))
    return jax.shard_map(shards, mesh=mesh, in_specs=in_specs, out_specs=out_specs, check_vma=False)
```

```python
import functools
import math

import jax
import jax.numpy as jnp
import numpy as np
from jax import lax
from jax.experimental import pallas as pl
from jax.experimental.pallas import tpu as pltpu
from jax.sharding import PartitionSpec as P

BF16 = jnp.bfloat16
F32 = jnp.float32
VMEM_BYTES = 24 * 1024 * 1024
RARE = 15


def fourier_tables(length):
    half = length // 2
    steps = np.arange(half)[:, None] * np.arange(length)[None, :] % length
    angle = steps * (2.0 * math.pi / length)
    sines = np.sin(angle)
    sines[0] = 1.0 - 2.0 * (np.arange(length) % 2)
    table = np.concatenate([np.cos(angle), sines], 0)

    def split(values):
        high = values.astype(np.float32).astype(jnp.bfloat16)
        low = (values - high.astype(np.float64)).astype(np.float32).astype(jnp.bfloat16)
        return np.stack([high, low])

    return np.concatenate([split(table), split(table.T)])


def pack_kernel(lesser_ref, greater_ref, out_ref):
    pieces, _, _, lanes = out_ref.shape
    width = lanes // 2
    for n in range(pieces):
        cols = slice(n * width, (n + 1) * width)
        out_ref[n] = jnp.concatenate([lesser_ref[:, :, cols], greater_ref[:, :, cols]], axis=-1)


def unpack_kernel(in_ref, lesser_ref, greater_ref):
    pieces, _, _, lanes = in_ref.shape
    width = lanes // 2
    per_tile = max(1, 128 // width)
    for first in range(0, pieces, per_tile):
        group = range(first, min(first + per_tile, pieces))
        cols = slice(first * width, (group[-1] + 1) * width)
        lesser_ref[:, :, cols] = jnp.concatenate([in_ref[n][:, :, :width] for n in group], axis=-1)
        greater_ref[:, :, cols] = jnp.concatenate([in_ref[n][:, :, width:] for n in group], axis=-1)


def one_hot(index_row, depth):
    rows = lax.broadcasted_iota(jnp.int32, (depth, index_row.shape[-1]), 0)
    return jnp.where(rows == index_row, 1.0, 0.0).astype(BF16)


def dot(a, b):
    return lax.dot_general(a, b, (((1,), (0,)), ((), ())), preferred_element_type=F32)


def rows_of(ref, part):
    blocks, _, energies, lanes = ref.shape
    return ref[:, part].reshape(blocks * energies, lanes)


def forward_sums(table_ref, signals):
    return dot(table_ref[0], signals) + dot(table_ref[1], signals)


def correlate(near, far, table_ref):
    half = near.shape[0] // 2
    length = near.shape[0]
    lanes = near.shape[1] // 2

    def parts(sums):
        return [sums[i * half : (i + 1) * half, j * lanes : (j + 1) * lanes] for i in range(2) for j in range(2)]

    a_re, a_im, b_re, b_im = parts(near)
    c_re, c_im, d_re, d_im = parts(far)
    first = lax.broadcasted_iota(jnp.int32, (half, lanes), 0) == 0
    ac_re, ac_im = a_re * c_re - a_im * c_im, a_re * c_im + a_im * c_re
    bd_re, bd_im = b_re * d_re - b_im * d_im, b_re * d_im + b_im * d_re
    u_re = jnp.where(first, 0.5 * ac_re, ac_re + bd_re)
    u_im = jnp.where(first, 0.5 * ac_im, ac_im + bd_im)
    v_re = jnp.where(first, 0.5 * bd_re, b_re * c_re - b_im * c_im - (a_re * d_re - a_im * d_im))
    v_im = jnp.where(first, 0.5 * bd_im, b_re * c_im + b_im * c_re - (a_re * d_im + a_im * d_re))
    top = jnp.concatenate([u_im, -u_re], axis=-1)
    bottom = jnp.concatenate([v_im, -v_re], axis=-1)
    products = jnp.concatenate([top, bottom], axis=0)
    high = products.astype(BF16)
    low = (products - high.astype(F32)).astype(BF16)
    back = dot(table_ref[2], high) + (dot(table_ref[2], low) + dot(table_ref[3], high))
    return (back * (2.0 / (length * math.sqrt(length)))).astype(BF16)


def correlate_kernel(index_ref, own_ref, far_ref, table_ref, out_ref):
    blocks, _, energies, lanes = own_ref.shape
    far = far_ref[...]
    own, partner = [], []
    for part in range(2):
        pick_far = one_hot(index_ref[part : part + 1, :], far.shape[-1])
        own.append(rows_of(own_ref, part))
        partner.append(dot(far, pick_far).astype(BF16))
    near = forward_sums(table_ref, jnp.concatenate(own, axis=-1))
    result = correlate(near, forward_sums(table_ref, jnp.concatenate(partner, axis=-1)), table_ref)
    for part in range(2):
        out_ref[:, part] = result[:, part * lanes : (part + 1) * lanes].reshape(blocks, energies, lanes)


def call(kernel, out_shape, flops, *args, scratch=(), in_hbm=(), out_smem=()):
    many = isinstance(out_shape, (list, tuple))
    outs = list(out_shape) if many else [out_shape]
    moved = sum(math.prod(v.shape) * v.dtype.itemsize for v in [*args, *outs])


    def specs(values, elsewhere, space):
        return [pl.BlockSpec(memory_space=space if i in elsewhere else pltpu.VMEM) for i in range(len(values))]

    out_specs = specs(outs, out_smem, pltpu.SMEM)
    args = [pltpu.with_memory_space_constraint(v, pltpu.HBM) if i in in_hbm else v for i, v in enumerate(args)]
    return pl.pallas_call(
        kernel,
        out_shape=out_shape,
        in_specs=specs(args, in_hbm, pltpu.HBM),
        out_specs=out_specs if many else out_specs[0],
        scratch_shapes=list(scratch),
        compiler_params=pltpu.CompilerParams(vmem_limit_bytes=VMEM_BYTES),
        cost_estimate=pl.CostEstimate(flops=flops, bytes_accessed=moved, transcendentals=0),
    )(*args)


def place():
    me = lax.axis_index("energy")
    return me // 2, me % 2


def columns_of(chip, width):
    return pl.ds(pl.multiple_of(chip * 2 * width, 2 * width), 2 * width)


def distances(lists_ref, plan_ref):
    pieces, groups, _ = lists_ref.shape
    group = lax.axis_index("elem")
    distance = []
    for n in range(pieces):
        found = jnp.int32(0)
        for i in range(groups):
            filled = lists_ref[n, i, 0] + lists_ref[n, i, 1] > 0
            found = found + jnp.where(jnp.logical_and(filled, group != i), group ^ i, 0)
        distance.append(found)
    near = [jnp.where(d == 1, 1, 0) for d in distance]
    middle = [jnp.where(d == 2, 1, 0) for d in distance]
    count_near, count_middle = sum(near), sum(middle)
    code = count_near * (pieces + 1) + count_middle
    number = jnp.int32(0)
    for i, (near_count, middle_count) in enumerate(counts_of(pieces)):
        number = jnp.where(code == near_count * (pieces + 1) + middle_count, i, number)
    seen_near, seen_middle, seen_far = jnp.int32(0), count_near, count_near + count_middle
    for n in range(pieces):
        far = 1 - near[n] - middle[n]
        rank = near[n] * seen_near + middle[n] * seen_middle + far * seen_far
        seen_near, seen_middle, seen_far = seen_near + near[n], seen_middle + middle[n], seen_far + far
        line = jnp.where(number < RARE, pieces - 1 - rank, 2 * (rank % (pieces // 2)) + rank // (pieces // 2))
        plan_ref[line] = jnp.int32(n)
        plan_ref[pieces + n] = line
    plan_ref[2 * pieces] = number


def counts_of(pieces):
    counts = [(near, middle) for near in range(pieces + 1) for middle in range(pieces + 1 - near)]
    return sorted(counts, key=lambda c: (math.comb(pieces, c[0]) * math.comb(pieces - c[0], c[1]), c))


def over_elem(number, values, after, *args):
    pieces, groups = lax.axis_size("energy"), lax.axis_size("elem")

    def branch(number, near, middle):
        ranked = [1] * near + [2] * middle + [3] * (pieces - near - middle)
        rank = [pieces - 1 - n if number < RARE else n // 2 + pieces // 2 * (n % 2) for n in range(pieces)]
        by_line = [ranked[rank[n]] for n in range(pieces)]
        pairs = [(n * groups + i, n * groups + (i ^ by_line[n])) for n in range(pieces) for i in range(groups)]
        return lambda sent, *args: after(lax.ppermute(sent, ("energy", "elem"), pairs), *args)

    return lax.switch(number, [branch(i, *counts) for i, counts in enumerate(counts_of(pieces))], values, *args)


def split_kernel(lists_ref, slots_ref, lesser_ref, greater_ref, *refs):
    (diagonal_ref, keep_ref, give_ref, number_ref, lines_ref, rows_ref, spots_ref) = refs[:7]
    lesser, greater, lists, slots, packed, scalars, plan_ref, sems = refs[7:]
    chip, core = place()
    pairs = [(lists_ref, scalars), (lists_ref, lists), (slots_ref, slots), (lesser_ref, lesser), (greater_ref, greater)]
    copies = [pltpu.make_async_copy(source, target, sems.at[i]) for i, (source, target) in enumerate(pairs)]
    for copy in copies:
        copy.start()
    for copy in copies[:3]:
        copy.wait()
    distances(scalars, plan_ref)
    pieces = packed.shape[0]
    number_ref[0] = plan_ref[2 * pieces]
    lines_ref[...] = jnp.full(lines_ref.shape, sum(plan_ref[pieces + n] * 8**n for n in range(pieces)), jnp.int32)
    piece = plan_ref[2 * chip + core]
    rows_ref[...] = lists[piece]
    spots_ref[0:1, :] = slots[pl.ds(piece // 2, 1), :]
    spots_ref[1:2, :] = jnp.full((1, spots_ref.shape[1]), piece % 2, jnp.int32)
    for copy in copies[3:]:
        copy.wait()
    width = packed.shape[-1] // 2
    for n in range(pieces):
        cols = slice(n * width, (n + 1) * width)
        packed[n] = jnp.concatenate([lesser[:, :, cols], greater[:, :, cols]], axis=-1)
    for which in range(2):
        diagonal_ref[which] = packed[plan_ref[2 * (chip ^ 3) + which]]
    for j in range(3):
        keep_ref[j] = packed[plan_ref[2 * (chip ^ j) + core]]
        give_ref[j] = packed[plan_ref[2 * (chip ^ j) + 1 - core]]


def swap(values, axis, bit):
    return lax.ppermute(values, axis, [(i, i ^ bit) for i in range(lax.axis_size(axis))])


def over_energy(diagonal, keep, give):
    diagonal = swap(diagonal, "energy", 6)
    got = swap(give, "energy", 1)
    beside = swap(jnp.stack([keep[2], got[2]]), "energy", 4)
    across = swap(jnp.stack([keep[1], got[1]]), "energy", 2)
    diagonal, beside = lax.optimization_barrier((diagonal, beside))
    return keep, got, diagonal, swap(diagonal, "energy", 1), beside, across


def blocks_of(refs, core):
    keep_ref, got_ref, diagonal_ref, diagonal_other_ref, beside_ref, across_ref = refs
    return [
        (lambda: keep_ref[0], lambda: got_ref[0]),
        (lambda: across_ref[0], lambda: across_ref[1]),
        (lambda: beside_ref[0], lambda: beside_ref[1]),
        (lambda: diagonal_ref[core], lambda: diagonal_other_ref[core]),
    ]


def lane_row(lanes):
    return lax.broadcasted_iota(jnp.int32, (1, lanes), 1)


def energies_of(device, energies):
    return pl.ds(pl.multiple_of(device * energies, energies), energies)


def repeat(values, index_row):
    return dot(values.astype(F32).astype(BF16), one_hot(index_row, values.shape[-1])).astype(jnp.int32)


def index_kernel(rows_ref, spots_ref, picks_ref):
    group = lax.axis_index("elem")
    lanes = picks_ref.shape[-1]
    width, cap = lanes // 2, lanes // 4
    lane = lane_row(lanes)
    lists = repeat(rows_ref[...], lane % cap)
    ids = lax.broadcasted_iota(jnp.int32, lists.shape, 0)
    greater = jnp.where(lane // cap % 2 == 1, width, 0)
    near_rows = jnp.sum(jnp.where(ids == group, lists, 0), axis=0, keepdims=True) + greater
    far_rows = jnp.sum(jnp.where(ids == group, 0, lists), axis=0, keepdims=True) + greater
    slots = spots_ref[0:1, :]
    twice = [repeat(slots, half * width + lane % width) for half in range(2)]
    slots = jnp.where(spots_ref[1:2, :] == 0, *twice)
    source = slots // cap
    spot = slots - source * cap + jnp.where(lane < width, cap, 0)
    near = one_hot(jnp.where(lane < 2 * cap, near_rows, -1), lanes)
    picks_ref[0] = dot(near, one_hot(jnp.where(source == group, spot, -1), lanes)).astype(BF16)
    for part in range(2):
        picks_ref[1 + part] = one_hot(jnp.where(source == group, -1, spot + 2 * cap * part), lanes)
        picks_ref[3 + part] = one_hot(jnp.where(lane // (2 * cap) == part, far_rows, -1), lanes)


def gather_kernel(picks_ref, *refs):
    in_refs, (signals_ref, sent_ref) = refs[:6], refs[6:]
    chip, core = place()
    energies, lanes = in_refs[0].shape[2:]
    for j, pair in enumerate(blocks_of(in_refs, core)):
        for which, block in enumerate(pair):
            values = block()
            rows = energies_of(2 * (chip ^ j) + (core if which == 0 else 1 - core), energies)
            for part in range(2):
                signals_ref[rows, part * lanes : (part + 1) * lanes] = values[part]
    sent_ref[...] = (dot(signals_ref[:, :lanes], picks_ref[3]) + dot(signals_ref[:, lanes:], picks_ref[4])).astype(BF16)


def own_kernel(signals_ref, picks_ref, table_ref, sums_ref, partner_ref, held_ref, sems):
    lanes = picks_ref.shape[-1]
    steps = sems.shape[0] // 4
    height = table_ref.shape[1] // steps
    copies = []
    for i in range(4 * steps):
        rows = pl.ds(i % steps * height, height)
        copies.append(pltpu.make_async_copy(table_ref.at[i // steps, rows], held_ref.at[i // steps, rows], sems.at[i]))
    for copy in copies:
        copy.start()
    for part in range(2):
        cols = slice(part * lanes, (part + 1) * lanes)
        partner_ref[:, cols] = dot(signals_ref[:, cols], picks_ref[0]).astype(BF16)
    for copy in copies:
        copy.wait()
    sums_ref[...] = forward_sums(held_ref, signals_ref[...])


def pick_kernel(near_ref, far_ref, picks_ref, partner_ref):
    lanes = picks_ref.shape[-1]
    far = far_ref[...]
    for part in range(2):
        cols = slice(part * lanes, (part + 1) * lanes)
        partner_ref[:, cols] = (near_ref[:, cols].astype(F32) + dot(far, picks_ref[1 + part])).astype(BF16)


def exchange_kernel(sums_ref, partner_ref, table_ref, *refs):
    (diagonal_ref, keep_ref, give_ref), (held,) = refs[:3], refs[3:]
    chip, core = place()
    energies, lanes = keep_ref.shape[2:]
    held[...] = correlate(sums_ref[...], forward_sums(table_ref, partner_ref[...]), table_ref)

    def block(j, core):
        rows = energies_of(2 * (chip ^ j) + core, energies)
        return [held[rows, part * lanes : (part + 1) * lanes] for part in range(2)]

    for which in range(2):
        diagonal_ref[which, 0], diagonal_ref[which, 1] = block(3, which)
    for j in range(3):
        keep_ref[j, 0], keep_ref[j, 1] = block(j, core)
        give_ref[j, 0], give_ref[j, 1] = block(j, 1 - core)


def join_kernel(lines_ref, *refs):
    in_refs, (lesser_ref, greater_ref, held) = refs[:6], refs[6:]
    chip, core = place()
    width = held.shape[-1] // 2
    for j, (mine, other) in enumerate(blocks_of(in_refs, core)):
        held[2 * (chip ^ j) + core] = mine()
        held[2 * (chip ^ j) + 1 - core] = other()
    lines = jnp.max(lines_ref[...])
    for n in range(0, held.shape[0], 2):
        even, odd = held[lines // 8**n % 8], held[lines // 8 ** (n + 1) % 8]
        cols = slice(n * width, (n + 2) * width)
        lesser_ref[:, :, cols] = jnp.concatenate([even[..., :width], odd[..., :width]], axis=-1)
        greater_ref[:, :, cols] = jnp.concatenate([even[..., width:], odd[..., width:]], axis=-1)


def four_chips(g_lesser, g_greater, send_rows, partner_slot):
    _, energies, group_rows = g_lesser.shape
    cap = send_rows.shape[-1]
    lanes = 4 * cap
    length = 8 * energies
    pair = jax.ShapeDtypeStruct((2, 2, energies, lanes), BF16)
    three = jax.ShapeDtypeStruct((3, 2, energies, lanes), BF16)
    leaving = [pair, three, three]
    column = jax.ShapeDtypeStruct((length, lanes), BF16)
    whole = jax.ShapeDtypeStruct((length, 2 * lanes), BF16)
    slots = partner_slot.reshape(4, lanes)
    table = jnp.asarray(fourier_tables(length))

    scratch = [
        pltpu.VMEM(g_lesser.shape, BF16),
        pltpu.VMEM(g_lesser.shape, BF16),
        pltpu.VMEM(send_rows.shape[1:], jnp.int32),
        pltpu.VMEM(slots.shape, jnp.int32),
        pltpu.VMEM((8, 2, energies, lanes), BF16),
        pltpu.SMEM(send_rows.shape[1:], jnp.int32),
        pltpu.SMEM((17,), jnp.int32),
        pltpu.SemaphoreType.DMA((5,)),
    ]
    more = [
        jax.ShapeDtypeStruct((1,), jnp.int32),
        jax.ShapeDtypeStruct((8, lanes), jnp.int32),
        jax.ShapeDtypeStruct((4, cap), jnp.int32),
        jax.ShapeDtypeStruct((2, lanes), jnp.int32),
    ]
    diagonal, keep, give, number, lines, rows, spots = call(
        split_kernel,
        leaving + more,
        2**24,
        send_rows[0],
        slots,
        g_lesser,
        g_greater,
        scratch=scratch,
        in_hbm=(0, 1, 2, 3),
        out_smem=(3,),
    )
    picks = call(index_kernel, jax.ShapeDtypeStruct((5, lanes, lanes), BF16), 2**24, rows, spots)
    diagonal, picks = lax.optimization_barrier((diagonal, picks))

    signals, sent = call(gather_kernel, [whole, column], 2**26, picks, *over_energy(diagonal, keep, give))

    def after(far, signals, picks, table):
        shapes = [jax.ShapeDtypeStruct(whole.shape, F32), whole, jax.ShapeDtypeStruct(table.shape, BF16)]
        sems = [pltpu.SemaphoreType.DMA((16,))]
        sums, near, held = call(own_kernel, shapes, 2**29, signals, picks, table, scratch=sems, in_hbm=(2,))
        return sums, call(pick_kernel, whole, 2**26, near, far, picks), held

    sums, partner, held = over_elem(number[0], sent, after, signals, picks, table)
    results = call(exchange_kernel, leaving, 2**30, sums, partner, held, scratch=[pltpu.VMEM(whole.shape, BF16)])
    out = jax.ShapeDtypeStruct((2, energies, group_rows), BF16)
    scratch = [pltpu.VMEM((8, 2, energies, lanes), BF16)]
    return tuple(call(join_kernel, [out, out], 0, lines, *over_energy(*results), scratch=scratch))


def any_mesh(g_lesser, g_greater, send_rows, partner_slot):
    piece = lax.axis_index("energy")
    pieces = lax.axis_size("energy")
    _, energies, group_rows = g_lesser.shape
    groups, cap = send_rows.shape[2:]
    width = group_rows // pieces
    lanes = 2 * width
    length = pieces * energies
    packed_shape = jax.ShapeDtypeStruct((pieces, 2, energies, lanes), BF16)
    packed = call(pack_kernel, packed_shape, 0, g_lesser, g_greater)
    own = lax.all_to_all(packed, "energy", split_axis=0, concat_axis=0, tiled=True)
    rows = lax.dynamic_index_in_dim(send_rows[0], piece, 0, keepdims=False).reshape(-1)
    slots = lax.dynamic_slice_in_dim(partner_slot, piece * width, width, 0)
    pick = (jnp.arange(width, dtype=jnp.int32)[:, None] == rows[None, :]).astype(BF16)
    split = own.reshape(pieces, 2, energies, 2, width)
    outgoing = jnp.einsum("pceds,sm->mpced", split, pick, preferred_element_type=F32).astype(BF16)
    incoming = lax.all_to_all(outgoing, "elem", split_axis=0, concat_axis=0, tiled=True)
    table_width = groups * cap
    far = jnp.transpose(incoming, (1, 3, 2, 4, 0)).reshape(length, 4 * table_width)
    index = jnp.concatenate([slots + table_width, slots])
    index = jnp.stack([index, index + 2 * table_width])
    result = call(
        correlate_kernel,
        packed_shape,
        2 * length * length * lanes * 14,
        index,
        own,
        far,
        jnp.asarray(fourier_tables(length)),
    )
    back = lax.all_to_all(result, "energy", split_axis=0, concat_axis=0, tiled=True)
    out = jax.ShapeDtypeStruct((2, energies, group_rows), BF16)
    return tuple(call(unpack_kernel, [out, out], 0, back))


def shards(g_lesser, g_greater, send_rows, partner_slot):
    _, pieces, groups, cap = send_rows.shape
    fits = pieces == 8 and groups == 4 and cap == 32 and partner_slot.shape[0] == 512
    path = four_chips if fits else any_mesh
    return path(g_lesser, g_greater, send_rows, partner_slot)


def solution(mesh):
    in_specs = (
        P(None, "energy", "elem"),
        P(None, "energy", "elem"),
        P("elem", None, None, None),
        P("elem"),
    )
    out_specs = (P(None, "energy", "elem"), P(None, "energy", "elem"))
    return jax.shard_map(shards, mesh=mesh, in_specs=in_specs, out_specs=out_specs, check_vma=False)
```

```python
import functools
import math

import jax
import jax.numpy as jnp
import numpy as np
from jax import lax
from jax.experimental import pallas as pl
from jax.experimental.pallas import tpu as pltpu
from jax.sharding import PartitionSpec as P

BF16 = jnp.bfloat16
F32 = jnp.float32
VMEM_BYTES = 24 * 1024 * 1024
COLLECT_FLOPS = 2**33
RARE = 15


def fourier_tables(length):
    half = length // 2
    steps = np.arange(half)[:, None] * np.arange(length)[None, :] % length
    angle = steps * (2.0 * math.pi / length)
    sines = np.sin(angle)
    sines[0] = 1.0 - 2.0 * (np.arange(length) % 2)
    table = np.concatenate([np.cos(angle), sines], 0)

    def split(values):
        high = values.astype(np.float32).astype(jnp.bfloat16)
        low = (values - high.astype(np.float64)).astype(np.float32).astype(jnp.bfloat16)
        return np.stack([high, low])

    return np.concatenate([split(table), split(table.T)])


def pack_kernel(lesser_ref, greater_ref, out_ref):
    pieces, _, _, lanes = out_ref.shape
    width = lanes // 2
    for n in range(pieces):
        cols = slice(n * width, (n + 1) * width)
        out_ref[n] = jnp.concatenate([lesser_ref[:, :, cols], greater_ref[:, :, cols]], axis=-1)


def unpack_kernel(in_ref, lesser_ref, greater_ref):
    pieces, _, _, lanes = in_ref.shape
    width = lanes // 2
    per_tile = max(1, 128 // width)
    for first in range(0, pieces, per_tile):
        group = range(first, min(first + per_tile, pieces))
        cols = slice(first * width, (group[-1] + 1) * width)
        lesser_ref[:, :, cols] = jnp.concatenate([in_ref[n][:, :, :width] for n in group], axis=-1)
        greater_ref[:, :, cols] = jnp.concatenate([in_ref[n][:, :, width:] for n in group], axis=-1)


def one_hot(index_row, depth):
    rows = lax.broadcasted_iota(jnp.int32, (depth, index_row.shape[-1]), 0)
    return jnp.where(rows == index_row, 1.0, 0.0).astype(BF16)


def dot(a, b):
    return lax.dot_general(a, b, (((1,), (0,)), ((), ())), preferred_element_type=F32)


def rows_of(ref, part):
    blocks, _, energies, lanes = ref.shape
    return ref[:, part].reshape(blocks * energies, lanes)


def forward_sums(table_ref, signals):
    return dot(table_ref[0], signals) + dot(table_ref[1], signals)


def correlate(near, far, table_ref):
    half = near.shape[0] // 2
    length = near.shape[0]
    lanes = near.shape[1] // 2

    def parts(sums):
        return [sums[i * half : (i + 1) * half, j * lanes : (j + 1) * lanes] for i in range(2) for j in range(2)]

    a_re, a_im, b_re, b_im = parts(near)
    c_re, c_im, d_re, d_im = parts(far)
    first = lax.broadcasted_iota(jnp.int32, (half, lanes), 0) == 0
    ac_re, ac_im = a_re * c_re - a_im * c_im, a_re * c_im + a_im * c_re
    bd_re, bd_im = b_re * d_re - b_im * d_im, b_re * d_im + b_im * d_re
    u_re = jnp.where(first, 0.5 * ac_re, ac_re + bd_re)
    u_im = jnp.where(first, 0.5 * ac_im, ac_im + bd_im)
    v_re = jnp.where(first, 0.5 * bd_re, b_re * c_re - b_im * c_im - (a_re * d_re - a_im * d_im))
    v_im = jnp.where(first, 0.5 * bd_im, b_re * c_im + b_im * c_re - (a_re * d_im + a_im * d_re))
    top = jnp.concatenate([u_im, -u_re], axis=-1)
    bottom = jnp.concatenate([v_im, -v_re], axis=-1)
    products = jnp.concatenate([top, bottom], axis=0)
    high = products.astype(BF16)
    low = (products - high.astype(F32)).astype(BF16)
    back = dot(table_ref[2], high) + (dot(table_ref[2], low) + dot(table_ref[3], high))
    return (back * (2.0 / (length * math.sqrt(length)))).astype(BF16)


def correlate_kernel(index_ref, own_ref, far_ref, table_ref, out_ref):
    blocks, _, energies, lanes = own_ref.shape
    far = far_ref[...]
    own, partner = [], []
    for part in range(2):
        pick_far = one_hot(index_ref[part : part + 1, :], far.shape[-1])
        own.append(rows_of(own_ref, part))
        partner.append(dot(far, pick_far).astype(BF16))
    near = forward_sums(table_ref, jnp.concatenate(own, axis=-1))
    result = correlate(near, forward_sums(table_ref, jnp.concatenate(partner, axis=-1)), table_ref)
    for part in range(2):
        out_ref[:, part] = result[:, part * lanes : (part + 1) * lanes].reshape(blocks, energies, lanes)


def call(kernel, out_shape, flops, *args, scratch=(), in_hbm=(), out_smem=()):
    many = isinstance(out_shape, (list, tuple))
    outs = list(out_shape) if many else [out_shape]
    moved = sum(math.prod(v.shape) * v.dtype.itemsize for v in [*args, *outs])


    def specs(values, elsewhere, space):
        return [pl.BlockSpec(memory_space=space if i in elsewhere else pltpu.VMEM) for i in range(len(values))]

    out_specs = specs(outs, out_smem, pltpu.SMEM)
    args = [pltpu.with_memory_space_constraint(v, pltpu.HBM) if i in in_hbm else v for i, v in enumerate(args)]
    return pl.pallas_call(
        kernel,
        out_shape=out_shape,
        in_specs=specs(args, in_hbm, pltpu.HBM),
        out_specs=out_specs if many else out_specs[0],
        scratch_shapes=list(scratch),
        compiler_params=pltpu.CompilerParams(vmem_limit_bytes=VMEM_BYTES),
        cost_estimate=pl.CostEstimate(flops=flops, bytes_accessed=moved, transcendentals=0),
    )(*args)


def place():
    me = lax.axis_index("energy")
    return me // 2, me % 2


def columns_of(chip, width):
    return pl.ds(pl.multiple_of(chip * 2 * width, 2 * width), 2 * width)


def distances(lists_ref, plan_ref):
    pieces, groups, _ = lists_ref.shape
    group = lax.axis_index("elem")
    distance = []
    for n in range(pieces):
        found = jnp.int32(0)
        for i in range(groups):
            filled = lists_ref[n, i, 0] + lists_ref[n, i, 1] > 0
            found = found + jnp.where(jnp.logical_and(filled, group != i), group ^ i, 0)
        distance.append(found)
    near = [jnp.where(d == 1, 1, 0) for d in distance]
    middle = [jnp.where(d == 2, 1, 0) for d in distance]
    count_near, count_middle = sum(near), sum(middle)
    code = count_near * (pieces + 1) + count_middle
    number = jnp.int32(0)
    for i, (near_count, middle_count) in enumerate(counts_of(pieces)):
        number = jnp.where(code == near_count * (pieces + 1) + middle_count, i, number)
    seen_near, seen_middle, seen_far = jnp.int32(0), count_near, count_near + count_middle
    for n in range(pieces):
        far = 1 - near[n] - middle[n]
        rank = near[n] * seen_near + middle[n] * seen_middle + far * seen_far
        seen_near, seen_middle, seen_far = seen_near + near[n], seen_middle + middle[n], seen_far + far
        line = jnp.where(number < RARE, pieces - 1 - rank, 2 * (rank % (pieces // 2)) + rank // (pieces // 2))
        plan_ref[line] = jnp.int32(n)
        plan_ref[pieces + n] = line
    plan_ref[2 * pieces] = number


def counts_of(pieces):
    counts = [(near, middle) for near in range(pieces + 1) for middle in range(pieces + 1 - near)]
    return sorted(counts, key=lambda c: (math.comb(pieces, c[0]) * math.comb(pieces - c[0], c[1]), c))


def over_elem(number, values, after, *args):
    pieces, groups = lax.axis_size("energy"), lax.axis_size("elem")

    def branch(number, near, middle):
        ranked = [1] * near + [2] * middle + [3] * (pieces - near - middle)
        rank = [pieces - 1 - n if number < RARE else n // 2 + pieces // 2 * (n % 2) for n in range(pieces)]
        by_line = [ranked[rank[n]] for n in range(pieces)]
        pairs = [(n * groups + i, n * groups + (i ^ by_line[n])) for n in range(pieces) for i in range(groups)]
        return lambda sent, *args: after(lax.ppermute(sent, ("energy", "elem"), pairs), *args)

    return lax.switch(number, [branch(i, *counts) for i, counts in enumerate(counts_of(pieces))], values, *args)


def split_kernel(lists_ref, slots_ref, lesser_ref, greater_ref, *refs):
    (beside_ref, keep_ref, give_ref, number_ref, lines_ref, rows_ref, spots_ref) = refs[:7]
    lesser, greater, lists, slots, packed, scalars, plan_ref, sems = refs[7:]
    chip, core = place()
    pairs = [(lists_ref, scalars), (lists_ref, lists), (slots_ref, slots)]
    tile = keep_ref.shape[-1]
    for first in range(0, lesser.shape[-1], tile):
        cols = pl.ds(first, tile)
        pairs += [(source.at[:, :, cols], target.at[:, :, cols]) for source, target in ((lesser_ref, lesser), (greater_ref, greater))]
    copies = [pltpu.make_async_copy(source, target, sems.at[i]) for i, (source, target) in enumerate(pairs)]
    for copy in copies:
        copy.start()
    for copy in copies[:3]:
        copy.wait()
    distances(scalars, plan_ref)
    pieces = packed.shape[0]
    number_ref[0] = plan_ref[2 * pieces]
    lines_ref[...] = jnp.full(lines_ref.shape, sum(plan_ref[pieces + n] * 8**n for n in range(pieces)), jnp.int32)
    piece = plan_ref[2 * chip + core]
    rows_ref[...] = lists[piece]
    spots_ref[0:1, :] = slots[pl.ds(piece // 2, 1), :]
    spots_ref[1:2, :] = jnp.full((1, spots_ref.shape[1]), piece % 2, jnp.int32)
    for copy in copies[3:]:
        copy.wait()
    width = packed.shape[-1] // 2
    for n in range(pieces):
        cols = slice(n * width, (n + 1) * width)
        packed[n] = jnp.concatenate([lesser[:, :, cols], greater[:, :, cols]], axis=-1)
    for which in range(2):
        beside_ref[which] = packed[plan_ref[2 * (chip ^ 2) + which]]
    for i, j in enumerate((0, 1, 3)):
        keep_ref[i] = packed[plan_ref[2 * (chip ^ j) + core]]
        give_ref[i] = packed[plan_ref[2 * (chip ^ j) + 1 - core]]


def swap(values, axis, bit):
    return lax.ppermute(values, axis, [(i, i ^ bit) for i in range(lax.axis_size(axis))])


def collect_kernel(keep_ref, got_ref, diagonal_ref, across_ref, out_ref):
    out_ref[0], out_ref[1] = keep_ref[0], got_ref[0]
    for which in range(2):
        out_ref[2 + which] = across_ref[which]
        out_ref[4 + which] = diagonal_ref[which]


def over_energy(first, keep, give):
    beside = swap(first, "energy", 4)
    got = swap(give, "energy", 1)
    diagonal = swap(jnp.stack([keep[2], got[2]]), "energy", 6)
    across = swap(jnp.stack([keep[1], got[1]]), "energy", 2)
    early = jax.ShapeDtypeStruct((6, *keep.shape[1:]), BF16)
    early = call(collect_kernel, early, COLLECT_FLOPS, keep, got, diagonal, across)
    return early, beside, swap(beside, "energy", 1)


def blocks_of(refs, core):
    early_ref, beside_ref, beside_other_ref = refs
    early = [(lambda i=i: early_ref[i], lambda i=i: early_ref[i + 1]) for i in (0, 2, 4)]
    return [early[0], early[1], (lambda: beside_ref[core], lambda: beside_other_ref[core]), early[2]]


def lane_row(lanes):
    return lax.broadcasted_iota(jnp.int32, (1, lanes), 1)


def energies_of(device, energies):
    return pl.ds(pl.multiple_of(device * energies, energies), energies)


def repeat(values, index_row):
    return dot(values.astype(F32).astype(BF16), one_hot(index_row, values.shape[-1])).astype(jnp.int32)


def index_kernel(rows_ref, spots_ref, picks_ref):
    group = lax.axis_index("elem")
    lanes = picks_ref.shape[-1]
    width, cap = lanes // 2, lanes // 4
    lane = lane_row(lanes)
    lists = repeat(rows_ref[...], lane % cap)
    ids = lax.broadcasted_iota(jnp.int32, lists.shape, 0)
    greater = jnp.where(lane // cap % 2 == 1, width, 0)
    near_rows = jnp.sum(jnp.where(ids == group, lists, 0), axis=0, keepdims=True) + greater
    far_rows = jnp.sum(jnp.where(ids == group, 0, lists), axis=0, keepdims=True) + greater
    slots = spots_ref[0:1, :]
    twice = [repeat(slots, half * width + lane % width) for half in range(2)]
    slots = jnp.where(spots_ref[1:2, :] == 0, *twice)
    source = slots // cap
    spot = slots - source * cap + jnp.where(lane < width, cap, 0)
    near = one_hot(jnp.where(lane < 2 * cap, near_rows, -1), lanes)
    picks_ref[0] = dot(near, one_hot(jnp.where(source == group, spot, -1), lanes)).astype(BF16)
    for part in range(2):
        picks_ref[1 + part] = one_hot(jnp.where(source == group, -1, spot + 2 * cap * part), lanes)
        picks_ref[3 + part] = one_hot(jnp.where(lane // (2 * cap) == part, far_rows, -1), lanes)


def gather_kernel(picks_ref, *refs):
    in_refs, (signals_ref, sent_ref) = refs[:3], refs[3:]
    chip, core = place()
    energies, lanes = in_refs[0].shape[2:]
    for j, pair in enumerate(blocks_of(in_refs, core)):
        for which, block in enumerate(pair):
            values = block()
            rows = energies_of(2 * (chip ^ j) + (core if which == 0 else 1 - core), energies)
            for part in range(2):
                signals_ref[rows, part * lanes : (part + 1) * lanes] = values[part]
    sent_ref[...] = (dot(signals_ref[:, :lanes], picks_ref[3]) + dot(signals_ref[:, lanes:], picks_ref[4])).astype(BF16)


def own_kernel(signals_ref, picks_ref, table_ref, sums_ref, partner_ref, held_ref, sems):
    lanes = picks_ref.shape[-1]
    steps = sems.shape[0] // 4
    height = table_ref.shape[1] // steps
    copies = []
    for i in range(4 * steps):
        rows = pl.ds(i % steps * height, height)
        copies.append(pltpu.make_async_copy(table_ref.at[i // steps, rows], held_ref.at[i // steps, rows], sems.at[i]))
    for copy in copies:
        copy.start()
    for part in range(2):
        cols = slice(part * lanes, (part + 1) * lanes)
        partner_ref[:, cols] = dot(signals_ref[:, cols], picks_ref[0]).astype(BF16)
    for copy in copies:
        copy.wait()
    sums_ref[...] = forward_sums(held_ref, signals_ref[...])


def pick_kernel(near_ref, far_ref, picks_ref, partner_ref):
    lanes = picks_ref.shape[-1]
    far = far_ref[...]
    for part in range(2):
        cols = slice(part * lanes, (part + 1) * lanes)
        partner_ref[:, cols] = (near_ref[:, cols].astype(F32) + dot(far, picks_ref[1 + part])).astype(BF16)


def exchange_kernel(sums_ref, partner_ref, table_ref, *refs):
    (beside_ref, keep_ref, give_ref), (held,) = refs[:3], refs[3:]
    chip, core = place()
    energies, lanes = keep_ref.shape[2:]
    held[...] = correlate(sums_ref[...], forward_sums(table_ref, partner_ref[...]), table_ref)

    def block(j, core):
        rows = energies_of(2 * (chip ^ j) + core, energies)
        return [held[rows, part * lanes : (part + 1) * lanes] for part in range(2)]

    for which in range(2):
        beside_ref[which, 0], beside_ref[which, 1] = block(2, which)
    for i, j in enumerate((0, 1, 3)):
        keep_ref[i, 0], keep_ref[i, 1] = block(j, core)
        give_ref[i, 0], give_ref[i, 1] = block(j, 1 - core)


def join_kernel(lines_ref, *refs):
    in_refs, (lesser_ref, greater_ref, held) = refs[:3], refs[3:]
    chip, core = place()
    width = held.shape[-1] // 2
    for j, (mine, other) in enumerate(blocks_of(in_refs, core)):
        held[2 * (chip ^ j) + core] = mine()
        held[2 * (chip ^ j) + 1 - core] = other()
    lines = jnp.max(lines_ref[...])
    for n in range(0, held.shape[0], 2):
        even, odd = held[lines // 8**n % 8], held[lines // 8 ** (n + 1) % 8]
        cols = slice(n * width, (n + 2) * width)
        lesser_ref[:, :, cols] = jnp.concatenate([even[..., :width], odd[..., :width]], axis=-1)
        greater_ref[:, :, cols] = jnp.concatenate([even[..., width:], odd[..., width:]], axis=-1)


def four_chips(g_lesser, g_greater, send_rows, partner_slot):
    _, energies, group_rows = g_lesser.shape
    cap = send_rows.shape[-1]
    lanes = 4 * cap
    length = 8 * energies
    pair = jax.ShapeDtypeStruct((2, 2, energies, lanes), BF16)
    three = jax.ShapeDtypeStruct((3, 2, energies, lanes), BF16)
    leaving = [pair, three, three]
    column = jax.ShapeDtypeStruct((length, lanes), BF16)
    whole = jax.ShapeDtypeStruct((length, 2 * lanes), BF16)
    slots = partner_slot.reshape(4, lanes)
    table = jnp.asarray(fourier_tables(length))

    scratch = [
        pltpu.VMEM(g_lesser.shape, BF16),
        pltpu.VMEM(g_lesser.shape, BF16),
        pltpu.VMEM(send_rows.shape[1:], jnp.int32),
        pltpu.VMEM(slots.shape, jnp.int32),
        pltpu.VMEM((8, 2, energies, lanes), BF16),
        pltpu.SMEM(send_rows.shape[1:], jnp.int32),
        pltpu.SMEM((17,), jnp.int32),
        pltpu.SemaphoreType.DMA((11,)),
    ]
    more = [
        jax.ShapeDtypeStruct((1,), jnp.int32),
        jax.ShapeDtypeStruct((8, lanes), jnp.int32),
        jax.ShapeDtypeStruct((4, cap), jnp.int32),
        jax.ShapeDtypeStruct((2, lanes), jnp.int32),
    ]
    beside, keep, give, number, lines, rows, spots = call(
        split_kernel,
        leaving + more,
        2**24,
        send_rows[0],
        slots,
        g_lesser,
        g_greater,
        scratch=scratch,
        in_hbm=(0, 1, 2, 3),
        out_smem=(3,),
    )
    picks = call(index_kernel, jax.ShapeDtypeStruct((5, lanes, lanes), BF16), 2**24, rows, spots)
    beside, picks = lax.optimization_barrier((beside, picks))

    signals, sent = call(gather_kernel, [whole, column], 2**26, picks, *over_energy(beside, keep, give))

    def after(far, signals, picks, table):
        shapes = [jax.ShapeDtypeStruct(whole.shape, F32), whole, jax.ShapeDtypeStruct(table.shape, BF16)]
        sems = [pltpu.SemaphoreType.DMA((16,))]
        sums, near, held = call(own_kernel, shapes, 2**29, signals, picks, table, scratch=sems, in_hbm=(2,))
        return sums, call(pick_kernel, whole, 2**26, near, far, picks), held

    sums, partner, held = over_elem(number[0], sent, after, signals, picks, table)
    results = call(exchange_kernel, leaving, 2**30, sums, partner, held, scratch=[pltpu.VMEM(whole.shape, BF16)])
    out = jax.ShapeDtypeStruct((2, energies, group_rows), BF16)
    scratch = [pltpu.VMEM((8, 2, energies, lanes), BF16)]
    return tuple(call(join_kernel, [out, out], 0, lines, *over_energy(*results), scratch=scratch))


def any_mesh(g_lesser, g_greater, send_rows, partner_slot):
    piece = lax.axis_index("energy")
    pieces = lax.axis_size("energy")
    _, energies, group_rows = g_lesser.shape
    groups, cap = send_rows.shape[2:]
    width = group_rows // pieces
    lanes = 2 * width
    length = pieces * energies
    packed_shape = jax.ShapeDtypeStruct((pieces, 2, energies, lanes), BF16)
    packed = call(pack_kernel, packed_shape, 0, g_lesser, g_greater)
    own = lax.all_to_all(packed, "energy", split_axis=0, concat_axis=0, tiled=True)
    rows = lax.dynamic_index_in_dim(send_rows[0], piece, 0, keepdims=False).reshape(-1)
    slots = lax.dynamic_slice_in_dim(partner_slot, piece * width, width, 0)
    pick = (jnp.arange(width, dtype=jnp.int32)[:, None] == rows[None, :]).astype(BF16)
    split = own.reshape(pieces, 2, energies, 2, width)
    outgoing = jnp.einsum("pceds,sm->mpced", split, pick, preferred_element_type=F32).astype(BF16)
    incoming = lax.all_to_all(outgoing, "elem", split_axis=0, concat_axis=0, tiled=True)
    table_width = groups * cap
    far = jnp.transpose(incoming, (1, 3, 2, 4, 0)).reshape(length, 4 * table_width)
    index = jnp.concatenate([slots + table_width, slots])
    index = jnp.stack([index, index + 2 * table_width])
    result = call(
        correlate_kernel,
        packed_shape,
        2 * length * length * lanes * 14,
        index,
        own,
        far,
        jnp.asarray(fourier_tables(length)),
    )
    back = lax.all_to_all(result, "energy", split_axis=0, concat_axis=0, tiled=True)
    out = jax.ShapeDtypeStruct((2, energies, group_rows), BF16)
    return tuple(call(unpack_kernel, [out, out], 0, back))


def shards(g_lesser, g_greater, send_rows, partner_slot):
    _, pieces, groups, cap = send_rows.shape
    fits = pieces == 8 and groups == 4 and cap == 32 and partner_slot.shape[0] == 512
    path = four_chips if fits else any_mesh
    return path(g_lesser, g_greater, send_rows, partner_slot)


def solution(mesh):
    in_specs = (
        P(None, "energy", "elem"),
        P(None, "energy", "elem"),
        P("elem", None, None, None),
        P("elem"),
    )
    out_specs = (P(None, "energy", "elem"), P(None, "energy", "elem"))
    return jax.shard_map(shards, mesh=mesh, in_specs=in_specs, out_specs=out_specs, check_vma=False)
```

```python
import functools
import math

import jax
import jax.numpy as jnp
import numpy as np
from jax import lax
from jax.experimental import pallas as pl
from jax.experimental.pallas import tpu as pltpu
from jax.sharding import PartitionSpec as P

BF16 = jnp.bfloat16
F32 = jnp.float32
VMEM_BYTES = 24 * 1024 * 1024
COLLECT_FLOPS = 2**33
RARE = 15


def fourier_tables(length):
    half = length // 2
    steps = np.arange(half)[:, None] * np.arange(length)[None, :] % length
    angle = steps * (2.0 * math.pi / length)
    sines = np.sin(angle)
    sines[0] = 1.0 - 2.0 * (np.arange(length) % 2)
    table = np.concatenate([np.cos(angle), sines], 0)

    def split(values):
        high = values.astype(np.float32).astype(jnp.bfloat16)
        low = (values - high.astype(np.float64)).astype(np.float32).astype(jnp.bfloat16)
        return np.stack([high, low])

    return np.concatenate([split(table), split(table.T)])


def pack_kernel(lesser_ref, greater_ref, out_ref):
    pieces, _, _, lanes = out_ref.shape
    width = lanes // 2
    for n in range(pieces):
        cols = slice(n * width, (n + 1) * width)
        out_ref[n] = jnp.concatenate([lesser_ref[:, :, cols], greater_ref[:, :, cols]], axis=-1)


def unpack_kernel(in_ref, lesser_ref, greater_ref):
    pieces, _, _, lanes = in_ref.shape
    width = lanes // 2
    per_tile = max(1, 128 // width)
    for first in range(0, pieces, per_tile):
        group = range(first, min(first + per_tile, pieces))
        cols = slice(first * width, (group[-1] + 1) * width)
        lesser_ref[:, :, cols] = jnp.concatenate([in_ref[n][:, :, :width] for n in group], axis=-1)
        greater_ref[:, :, cols] = jnp.concatenate([in_ref[n][:, :, width:] for n in group], axis=-1)


def one_hot(index_row, depth):
    rows = lax.broadcasted_iota(jnp.int32, (depth, index_row.shape[-1]), 0)
    return jnp.where(rows == index_row, 1.0, 0.0).astype(BF16)


def dot(a, b):
    return lax.dot_general(a, b, (((1,), (0,)), ((), ())), preferred_element_type=F32)


def rows_of(ref, part):
    blocks, _, energies, lanes = ref.shape
    return ref[:, part].reshape(blocks * energies, lanes)


def forward_sums(table_ref, signals):
    return dot(table_ref[0], signals) + dot(table_ref[1], signals)


def correlate(near, far, table_ref):
    half = near.shape[0] // 2
    length = near.shape[0]
    lanes = near.shape[1] // 2

    def parts(sums):
        return [sums[i * half : (i + 1) * half, j * lanes : (j + 1) * lanes] for i in range(2) for j in range(2)]

    a_re, a_im, b_re, b_im = parts(near)
    c_re, c_im, d_re, d_im = parts(far)
    first = lax.broadcasted_iota(jnp.int32, (half, lanes), 0) == 0
    ac_re, ac_im = a_re * c_re - a_im * c_im, a_re * c_im + a_im * c_re
    bd_re, bd_im = b_re * d_re - b_im * d_im, b_re * d_im + b_im * d_re
    u_re = jnp.where(first, 0.5 * ac_re, ac_re + bd_re)
    u_im = jnp.where(first, 0.5 * ac_im, ac_im + bd_im)
    v_re = jnp.where(first, 0.5 * bd_re, b_re * c_re - b_im * c_im - (a_re * d_re - a_im * d_im))
    v_im = jnp.where(first, 0.5 * bd_im, b_re * c_im + b_im * c_re - (a_re * d_im + a_im * d_re))
    top = jnp.concatenate([u_im, -u_re], axis=-1)
    bottom = jnp.concatenate([v_im, -v_re], axis=-1)
    products = jnp.concatenate([top, bottom], axis=0)
    high = products.astype(BF16)
    low = (products - high.astype(F32)).astype(BF16)
    back = dot(table_ref[2], high) + (dot(table_ref[2], low) + dot(table_ref[3], high))
    return (back * (2.0 / (length * math.sqrt(length)))).astype(BF16)


def correlate_kernel(index_ref, own_ref, far_ref, table_ref, out_ref):
    blocks, _, energies, lanes = own_ref.shape
    far = far_ref[...]
    own, partner = [], []
    for part in range(2):
        pick_far = one_hot(index_ref[part : part + 1, :], far.shape[-1])
        own.append(rows_of(own_ref, part))
        partner.append(dot(far, pick_far).astype(BF16))
    near = forward_sums(table_ref, jnp.concatenate(own, axis=-1))
    result = correlate(near, forward_sums(table_ref, jnp.concatenate(partner, axis=-1)), table_ref)
    for part in range(2):
        out_ref[:, part] = result[:, part * lanes : (part + 1) * lanes].reshape(blocks, energies, lanes)


def call(kernel, out_shape, flops, *args, scratch=(), in_hbm=(), out_smem=()):
    many = isinstance(out_shape, (list, tuple))
    outs = list(out_shape) if many else [out_shape]
    moved = sum(math.prod(v.shape) * v.dtype.itemsize for v in [*args, *outs])


    def specs(values, elsewhere, space):
        return [pl.BlockSpec(memory_space=space if i in elsewhere else pltpu.VMEM) for i in range(len(values))]

    out_specs = specs(outs, out_smem, pltpu.SMEM)
    args = [pltpu.with_memory_space_constraint(v, pltpu.HBM) if i in in_hbm else v for i, v in enumerate(args)]
    return pl.pallas_call(
        kernel,
        out_shape=out_shape,
        in_specs=specs(args, in_hbm, pltpu.HBM),
        out_specs=out_specs if many else out_specs[0],
        scratch_shapes=list(scratch),
        compiler_params=pltpu.CompilerParams(vmem_limit_bytes=VMEM_BYTES),
        cost_estimate=pl.CostEstimate(flops=flops, bytes_accessed=moved, transcendentals=0),
    )(*args)


def place():
    me = lax.axis_index("energy")
    return me // 2, me % 2


def columns_of(chip, width):
    return pl.ds(pl.multiple_of(chip * 2 * width, 2 * width), 2 * width)


def distances(lists_ref, plan_ref):
    pieces, groups, _ = lists_ref.shape
    group = lax.axis_index("elem")
    distance = []
    for n in range(pieces):
        found = jnp.int32(0)
        for i in range(groups):
            filled = lists_ref[n, i, 0] + lists_ref[n, i, 1] > 0
            found = found + jnp.where(jnp.logical_and(filled, group != i), group ^ i, 0)
        distance.append(found)
    near = [jnp.where(d == 1, 1, 0) for d in distance]
    middle = [jnp.where(d == 2, 1, 0) for d in distance]
    count_near, count_middle = sum(near), sum(middle)
    code = count_near * (pieces + 1) + count_middle
    number = jnp.int32(0)
    for i, (near_count, middle_count) in enumerate(counts_of(pieces)):
        number = jnp.where(code == near_count * (pieces + 1) + middle_count, i, number)
    seen_near, seen_middle, seen_far = jnp.int32(0), count_near, count_near + count_middle
    for n in range(pieces):
        far = 1 - near[n] - middle[n]
        rank = near[n] * seen_near + middle[n] * seen_middle + far * seen_far
        seen_near, seen_middle, seen_far = seen_near + near[n], seen_middle + middle[n], seen_far + far
        line = jnp.where(number < RARE, pieces - 1 - rank, 2 * (rank % (pieces // 2)) + 1 - rank // (pieces // 2))
        plan_ref[line] = jnp.int32(n)
        plan_ref[pieces + n] = line
    plan_ref[2 * pieces] = number


def counts_of(pieces):
    counts = [(near, middle) for near in range(pieces + 1) for middle in range(pieces + 1 - near)]
    return sorted(counts, key=lambda c: (math.comb(pieces, c[0]) * math.comb(pieces - c[0], c[1]), c))


def over_elem(number, values, after, *args):
    pieces, groups = lax.axis_size("energy"), lax.axis_size("elem")

    def branch(number, near, middle):
        ranked = [1] * near + [2] * middle + [3] * (pieces - near - middle)
        rank = [pieces - 1 - n if number < RARE else n // 2 + pieces // 2 * (1 - n % 2) for n in range(pieces)]
        by_line = [ranked[rank[n]] for n in range(pieces)]
        pairs = [(n * groups + i, n * groups + (i ^ by_line[n])) for n in range(pieces) for i in range(groups)]
        return lambda sent, *args: after(lax.ppermute(sent, ("energy", "elem"), pairs), *args)

    return lax.switch(number, [branch(i, *counts) for i, counts in enumerate(counts_of(pieces))], values, *args)


def split_kernel(lists_ref, slots_ref, lesser_ref, greater_ref, *refs):
    (beside_ref, keep_ref, give_ref, number_ref, lines_ref, rows_ref, spots_ref) = refs[:7]
    lesser, greater, lists, slots, packed, scalars, plan_ref, sems = refs[7:]
    chip, core = place()
    pairs = [(lists_ref, scalars), (lists_ref, lists), (slots_ref, slots)]
    tile = keep_ref.shape[-1]
    for first in range(0, lesser.shape[-1], tile):
        cols = pl.ds(first, tile)
        pairs += [(source.at[:, :, cols], target.at[:, :, cols]) for source, target in ((lesser_ref, lesser), (greater_ref, greater))]
    copies = [pltpu.make_async_copy(source, target, sems.at[i]) for i, (source, target) in enumerate(pairs)]
    for copy in copies:
        copy.start()
    for copy in copies[:3]:
        copy.wait()
    distances(scalars, plan_ref)
    pieces = packed.shape[0]
    number_ref[0] = plan_ref[2 * pieces]
    lines_ref[...] = jnp.full(lines_ref.shape, sum(plan_ref[pieces + n] * 8**n for n in range(pieces)), jnp.int32)
    piece = plan_ref[2 * chip + core]
    rows_ref[...] = lists[piece]
    spots_ref[0:1, :] = slots[pl.ds(piece // 2, 1), :]
    spots_ref[1:2, :] = jnp.full((1, spots_ref.shape[1]), piece % 2, jnp.int32)
    for copy in copies[3:]:
        copy.wait()
    width = packed.shape[-1] // 2
    for n in range(pieces):
        cols = slice(n * width, (n + 1) * width)
        packed[n] = jnp.concatenate([lesser[:, :, cols], greater[:, :, cols]], axis=-1)
    for which in range(2):
        beside_ref[which] = packed[plan_ref[2 * (chip ^ 2) + which]]
    for i, j in enumerate((0, 1, 3)):
        keep_ref[i] = packed[plan_ref[2 * (chip ^ j) + core]]
        give_ref[i] = packed[plan_ref[2 * (chip ^ j) + 1 - core]]


def swap(values, axis, bit):
    return lax.ppermute(values, axis, [(i, i ^ bit) for i in range(lax.axis_size(axis))])


def collect_kernel(keep_ref, got_ref, diagonal_ref, across_ref, out_ref):
    out_ref[0], out_ref[1] = keep_ref[0], got_ref[0]
    for which in range(2):
        out_ref[2 + which] = across_ref[which]
        out_ref[4 + which] = diagonal_ref[which]


def over_energy(first, keep, give):
    beside = swap(first, "energy", 4)
    got = swap(give, "energy", 1)
    diagonal = swap(jnp.stack([keep[2], got[2]]), "energy", 6)
    across = swap(jnp.stack([keep[1], got[1]]), "energy", 2)
    early = jax.ShapeDtypeStruct((6, *keep.shape[1:]), BF16)
    early = call(collect_kernel, early, COLLECT_FLOPS, keep, got, diagonal, across)
    return early, beside, swap(beside, "energy", 1)


def blocks_of(refs, core):
    early_ref, beside_ref, beside_other_ref = refs
    early = [(lambda i=i: early_ref[i], lambda i=i: early_ref[i + 1]) for i in (0, 2, 4)]
    return [early[0], early[1], (lambda: beside_ref[core], lambda: beside_other_ref[core]), early[2]]


def lane_row(lanes):
    return lax.broadcasted_iota(jnp.int32, (1, lanes), 1)


def energies_of(device, energies):
    return pl.ds(pl.multiple_of(device * energies, energies), energies)


def repeat(values, index_row):
    return dot(values.astype(F32).astype(BF16), one_hot(index_row, values.shape[-1])).astype(jnp.int32)


def index_kernel(rows_ref, spots_ref, picks_ref):
    group = lax.axis_index("elem")
    lanes = picks_ref.shape[-1]
    width, cap = lanes // 2, lanes // 4
    lane = lane_row(lanes)
    lists = repeat(rows_ref[...], lane % cap)
    ids = lax.broadcasted_iota(jnp.int32, lists.shape, 0)
    greater = jnp.where(lane // cap % 2 == 1, width, 0)
    near_rows = jnp.sum(jnp.where(ids == group, lists, 0), axis=0, keepdims=True) + greater
    far_rows = jnp.sum(jnp.where(ids == group, 0, lists), axis=0, keepdims=True) + greater
    slots = spots_ref[0:1, :]
    twice = [repeat(slots, half * width + lane % width) for half in range(2)]
    slots = jnp.where(spots_ref[1:2, :] == 0, *twice)
    source = slots // cap
    spot = slots - source * cap + jnp.where(lane < width, cap, 0)
    near = one_hot(jnp.where(lane < 2 * cap, near_rows, -1), lanes)
    picks_ref[0] = dot(near, one_hot(jnp.where(source == group, spot, -1), lanes)).astype(BF16)
    for part in range(2):
        picks_ref[1 + part] = one_hot(jnp.where(source == group, -1, spot + 2 * cap * part), lanes)
        picks_ref[3 + part] = one_hot(jnp.where(lane // (2 * cap) == part, far_rows, -1), lanes)


def gather_kernel(picks_ref, *refs):
    in_refs, (signals_ref, sent_ref) = refs[:3], refs[3:]
    chip, core = place()
    energies, lanes = in_refs[0].shape[2:]
    for j, pair in enumerate(blocks_of(in_refs, core)):
        for which, block in enumerate(pair):
            values = block()
            rows = energies_of(2 * (chip ^ j) + (core if which == 0 else 1 - core), energies)
            for part in range(2):
                signals_ref[rows, part * lanes : (part + 1) * lanes] = values[part]
    sent_ref[...] = (dot(signals_ref[:, :lanes], picks_ref[3]) + dot(signals_ref[:, lanes:], picks_ref[4])).astype(BF16)


def own_kernel(signals_ref, picks_ref, table_ref, sums_ref, partner_ref, held_ref, sems):
    lanes = picks_ref.shape[-1]
    steps = sems.shape[0] // 4
    height = table_ref.shape[1] // steps
    copies = []
    for i in range(4 * steps):
        rows = pl.ds(i % steps * height, height)
        copies.append(pltpu.make_async_copy(table_ref.at[i // steps, rows], held_ref.at[i // steps, rows], sems.at[i]))
    for copy in copies:
        copy.start()
    for part in range(2):
        cols = slice(part * lanes, (part + 1) * lanes)
        partner_ref[:, cols] = dot(signals_ref[:, cols], picks_ref[0]).astype(BF16)
    for copy in copies:
        copy.wait()
    sums_ref[...] = forward_sums(held_ref, signals_ref[...])


def pick_kernel(near_ref, far_ref, picks_ref, partner_ref):
    lanes = picks_ref.shape[-1]
    far = far_ref[...]
    for part in range(2):
        cols = slice(part * lanes, (part + 1) * lanes)
        partner_ref[:, cols] = (near_ref[:, cols].astype(F32) + dot(far, picks_ref[1 + part])).astype(BF16)


def exchange_kernel(sums_ref, partner_ref, table_ref, *refs):
    (beside_ref, keep_ref, give_ref), (held,) = refs[:3], refs[3:]
    chip, core = place()
    energies, lanes = keep_ref.shape[2:]
    held[...] = correlate(sums_ref[...], forward_sums(table_ref, partner_ref[...]), table_ref)

    def block(j, core):
        rows = energies_of(2 * (chip ^ j) + core, energies)
        return [held[rows, part * lanes : (part + 1) * lanes] for part in range(2)]

    for which in range(2):
        beside_ref[which, 0], beside_ref[which, 1] = block(2, which)
    for i, j in enumerate((0, 1, 3)):
        keep_ref[i, 0], keep_ref[i, 1] = block(j, core)
        give_ref[i, 0], give_ref[i, 1] = block(j, 1 - core)


def join_kernel(lines_ref, *refs):
    in_refs, (lesser_ref, greater_ref, held) = refs[:3], refs[3:]
    chip, core = place()
    width = held.shape[-1] // 2
    for j, (mine, other) in enumerate(blocks_of(in_refs, core)):
        held[2 * (chip ^ j) + core] = mine()
        held[2 * (chip ^ j) + 1 - core] = other()
    lines = jnp.max(lines_ref[...])
    for n in range(0, held.shape[0], 2):
        even, odd = held[lines // 8**n % 8], held[lines // 8 ** (n + 1) % 8]
        cols = slice(n * width, (n + 2) * width)
        lesser_ref[:, :, cols] = jnp.concatenate([even[..., :width], odd[..., :width]], axis=-1)
        greater_ref[:, :, cols] = jnp.concatenate([even[..., width:], odd[..., width:]], axis=-1)


def four_chips(g_lesser, g_greater, send_rows, partner_slot):
    _, energies, group_rows = g_lesser.shape
    cap = send_rows.shape[-1]
    lanes = 4 * cap
    length = 8 * energies
    pair = jax.ShapeDtypeStruct((2, 2, energies, lanes), BF16)
    three = jax.ShapeDtypeStruct((3, 2, energies, lanes), BF16)
    leaving = [pair, three, three]
    column = jax.ShapeDtypeStruct((length, lanes), BF16)
    whole = jax.ShapeDtypeStruct((length, 2 * lanes), BF16)
    slots = partner_slot.reshape(4, lanes)
    table = jnp.asarray(fourier_tables(length))

    scratch = [
        pltpu.VMEM(g_lesser.shape, BF16),
        pltpu.VMEM(g_lesser.shape, BF16),
        pltpu.VMEM(send_rows.shape[1:], jnp.int32),
        pltpu.VMEM(slots.shape, jnp.int32),
        pltpu.VMEM((8, 2, energies, lanes), BF16),
        pltpu.SMEM(send_rows.shape[1:], jnp.int32),
        pltpu.SMEM((17,), jnp.int32),
        pltpu.SemaphoreType.DMA((11,)),
    ]
    more = [
        jax.ShapeDtypeStruct((1,), jnp.int32),
        jax.ShapeDtypeStruct((8, lanes), jnp.int32),
        jax.ShapeDtypeStruct((4, cap), jnp.int32),
        jax.ShapeDtypeStruct((2, lanes), jnp.int32),
    ]
    beside, keep, give, number, lines, rows, spots = call(
        split_kernel,
        leaving + more,
        2**24,
        send_rows[0],
        slots,
        g_lesser,
        g_greater,
        scratch=scratch,
        in_hbm=(0, 1, 2, 3),
        out_smem=(3,),
    )
    picks = call(index_kernel, jax.ShapeDtypeStruct((5, lanes, lanes), BF16), 2**24, rows, spots)
    beside, picks = lax.optimization_barrier((beside, picks))

    signals, sent = call(gather_kernel, [whole, column], 2**26, picks, *over_energy(beside, keep, give))

    def after(far, signals, picks, table):
        shapes = [jax.ShapeDtypeStruct(whole.shape, F32), whole, jax.ShapeDtypeStruct(table.shape, BF16)]
        sems = [pltpu.SemaphoreType.DMA((16,))]
        sums, near, held = call(own_kernel, shapes, 2**29, signals, picks, table, scratch=sems, in_hbm=(2,))
        return sums, call(pick_kernel, whole, 2**26, near, far, picks), held

    sums, partner, held = over_elem(number[0], sent, after, signals, picks, table)
    results = call(exchange_kernel, leaving, 2**30, sums, partner, held, scratch=[pltpu.VMEM(whole.shape, BF16)])
    out = jax.ShapeDtypeStruct((2, energies, group_rows), BF16)
    scratch = [pltpu.VMEM((8, 2, energies, lanes), BF16)]
    return tuple(call(join_kernel, [out, out], 0, lines, *over_energy(*results), scratch=scratch))


def any_mesh(g_lesser, g_greater, send_rows, partner_slot):
    piece = lax.axis_index("energy")
    pieces = lax.axis_size("energy")
    _, energies, group_rows = g_lesser.shape
    groups, cap = send_rows.shape[2:]
    width = group_rows // pieces
    lanes = 2 * width
    length = pieces * energies
    packed_shape = jax.ShapeDtypeStruct((pieces, 2, energies, lanes), BF16)
    packed = call(pack_kernel, packed_shape, 0, g_lesser, g_greater)
    own = lax.all_to_all(packed, "energy", split_axis=0, concat_axis=0, tiled=True)
    rows = lax.dynamic_index_in_dim(send_rows[0], piece, 0, keepdims=False).reshape(-1)
    slots = lax.dynamic_slice_in_dim(partner_slot, piece * width, width, 0)
    pick = (jnp.arange(width, dtype=jnp.int32)[:, None] == rows[None, :]).astype(BF16)
    split = own.reshape(pieces, 2, energies, 2, width)
    outgoing = jnp.einsum("pceds,sm->mpced", split, pick, preferred_element_type=F32).astype(BF16)
    incoming = lax.all_to_all(outgoing, "elem", split_axis=0, concat_axis=0, tiled=True)
    table_width = groups * cap
    far = jnp.transpose(incoming, (1, 3, 2, 4, 0)).reshape(length, 4 * table_width)
    index = jnp.concatenate([slots + table_width, slots])
    index = jnp.stack([index, index + 2 * table_width])
    result = call(
        correlate_kernel,
        packed_shape,
        2 * length * length * lanes * 14,
        index,
        own,
        far,
        jnp.asarray(fourier_tables(length)),
    )
    back = lax.all_to_all(result, "energy", split_axis=0, concat_axis=0, tiled=True)
    out = jax.ShapeDtypeStruct((2, energies, group_rows), BF16)
    return tuple(call(unpack_kernel, [out, out], 0, back))


def shards(g_lesser, g_greater, send_rows, partner_slot):
    _, pieces, groups, cap = send_rows.shape
    fits = pieces == 8 and groups == 4 and cap == 32 and partner_slot.shape[0] == 512
    path = four_chips if fits else any_mesh
    return path(g_lesser, g_greater, send_rows, partner_slot)


def solution(mesh):
    in_specs = (
        P(None, "energy", "elem"),
        P(None, "energy", "elem"),
        P("elem", None, None, None),
        P("elem"),
    )
    out_specs = (P(None, "energy", "elem"), P(None, "energy", "elem"))
    return jax.shard_map(shards, mesh=mesh, in_specs=in_specs, out_specs=out_specs, check_vma=False)
```

```python
import functools
import math

import jax
import jax.numpy as jnp
import numpy as np
from jax import lax
from jax.experimental import pallas as pl
from jax.experimental.pallas import tpu as pltpu
from jax.sharding import PartitionSpec as P

BF16 = jnp.bfloat16
F32 = jnp.float32
VMEM_BYTES = 24 * 1024 * 1024
COLLECT_FLOPS = 2**33
RARE = 15


def fourier_tables(length):
    half = length // 2
    steps = np.arange(half)[:, None] * np.arange(length)[None, :] % length
    angle = steps * (2.0 * math.pi / length)
    sines = np.sin(angle)
    sines[0] = 1.0 - 2.0 * (np.arange(length) % 2)
    table = np.concatenate([np.cos(angle), sines], 0)

    def split(values):
        high = values.astype(np.float32).astype(jnp.bfloat16)
        low = (values - high.astype(np.float64)).astype(np.float32).astype(jnp.bfloat16)
        return np.stack([high, low])

    return np.concatenate([split(table), split(table.T)])


def pack_kernel(lesser_ref, greater_ref, out_ref):
    pieces, _, _, lanes = out_ref.shape
    width = lanes // 2
    for n in range(pieces):
        cols = slice(n * width, (n + 1) * width)
        out_ref[n] = jnp.concatenate([lesser_ref[:, :, cols], greater_ref[:, :, cols]], axis=-1)


def unpack_kernel(in_ref, lesser_ref, greater_ref):
    pieces, _, _, lanes = in_ref.shape
    width = lanes // 2
    per_tile = max(1, 128 // width)
    for first in range(0, pieces, per_tile):
        group = range(first, min(first + per_tile, pieces))
        cols = slice(first * width, (group[-1] + 1) * width)
        lesser_ref[:, :, cols] = jnp.concatenate([in_ref[n][:, :, :width] for n in group], axis=-1)
        greater_ref[:, :, cols] = jnp.concatenate([in_ref[n][:, :, width:] for n in group], axis=-1)


def one_hot(index_row, depth):
    rows = lax.broadcasted_iota(jnp.int32, (depth, index_row.shape[-1]), 0)
    return jnp.where(rows == index_row, 1.0, 0.0).astype(BF16)


def dot(a, b):
    return lax.dot_general(a, b, (((1,), (0,)), ((), ())), preferred_element_type=F32)


def rows_of(ref, part):
    blocks, _, energies, lanes = ref.shape
    return ref[:, part].reshape(blocks * energies, lanes)


def forward_sums(table_ref, signals):
    return dot(table_ref[0], signals) + dot(table_ref[1], signals)


def correlate(near, far, table_ref):
    half = near.shape[0] // 2
    length = near.shape[0]
    lanes = near.shape[1] // 2

    def parts(sums):
        return [sums[i * half : (i + 1) * half, j * lanes : (j + 1) * lanes] for i in range(2) for j in range(2)]

    a_re, a_im, b_re, b_im = parts(near)
    c_re, c_im, d_re, d_im = parts(far)
    first = lax.broadcasted_iota(jnp.int32, (half, lanes), 0) == 0
    ac_re, ac_im = a_re * c_re - a_im * c_im, a_re * c_im + a_im * c_re
    bd_re, bd_im = b_re * d_re - b_im * d_im, b_re * d_im + b_im * d_re
    u_re = jnp.where(first, 0.5 * ac_re, ac_re + bd_re)
    u_im = jnp.where(first, 0.5 * ac_im, ac_im + bd_im)
    v_re = jnp.where(first, 0.5 * bd_re, b_re * c_re - b_im * c_im - (a_re * d_re - a_im * d_im))
    v_im = jnp.where(first, 0.5 * bd_im, b_re * c_im + b_im * c_re - (a_re * d_im + a_im * d_re))
    top = jnp.concatenate([u_im, -u_re], axis=-1)
    bottom = jnp.concatenate([v_im, -v_re], axis=-1)
    products = jnp.concatenate([top, bottom], axis=0)
    high = products.astype(BF16)
    low = (products - high.astype(F32)).astype(BF16)
    back = dot(table_ref[2], high) + (dot(table_ref[2], low) + dot(table_ref[3], high))
    return (back * (2.0 / (length * math.sqrt(length)))).astype(BF16)


def correlate_kernel(index_ref, own_ref, far_ref, table_ref, out_ref):
    blocks, _, energies, lanes = own_ref.shape
    far = far_ref[...]
    own, partner = [], []
    for part in range(2):
        pick_far = one_hot(index_ref[part : part + 1, :], far.shape[-1])
        own.append(rows_of(own_ref, part))
        partner.append(dot(far, pick_far).astype(BF16))
    near = forward_sums(table_ref, jnp.concatenate(own, axis=-1))
    result = correlate(near, forward_sums(table_ref, jnp.concatenate(partner, axis=-1)), table_ref)
    for part in range(2):
        out_ref[:, part] = result[:, part * lanes : (part + 1) * lanes].reshape(blocks, energies, lanes)


def call(kernel, out_shape, flops, *args, scratch=(), in_hbm=(), out_smem=()):
    many = isinstance(out_shape, (list, tuple))
    outs = list(out_shape) if many else [out_shape]
    moved = sum(math.prod(v.shape) * v.dtype.itemsize for v in [*args, *outs])


    def specs(values, elsewhere, space):
        return [pl.BlockSpec(memory_space=space if i in elsewhere else pltpu.VMEM) for i in range(len(values))]

    out_specs = specs(outs, out_smem, pltpu.SMEM)
    args = [pltpu.with_memory_space_constraint(v, pltpu.HBM) if i in in_hbm else v for i, v in enumerate(args)]
    return pl.pallas_call(
        kernel,
        out_shape=out_shape,
        in_specs=specs(args, in_hbm, pltpu.HBM),
        out_specs=out_specs if many else out_specs[0],
        scratch_shapes=list(scratch),
        compiler_params=pltpu.CompilerParams(vmem_limit_bytes=VMEM_BYTES),
        cost_estimate=pl.CostEstimate(flops=flops, bytes_accessed=moved, transcendentals=0),
    )(*args)


def place():
    me = lax.axis_index("energy")
    return me // 2, me % 2


def columns_of(chip, width):
    return pl.ds(pl.multiple_of(chip * 2 * width, 2 * width), 2 * width)


def distances(lists_ref, plan_ref):
    pieces, groups, _ = lists_ref.shape
    group = lax.axis_index("elem")
    distance = []
    for n in range(pieces):
        found = jnp.int32(0)
        for i in range(groups):
            filled = lists_ref[n, i, 0] + lists_ref[n, i, 1] > 0
            found = found + jnp.where(jnp.logical_and(filled, group != i), group ^ i, 0)
        distance.append(found)
    near = [jnp.where(d == 1, 1, 0) for d in distance]
    middle = [jnp.where(d == 2, 1, 0) for d in distance]
    count_near, count_middle = sum(near), sum(middle)
    code = count_near * (pieces + 1) + count_middle
    number = jnp.int32(0)
    for i, (near_count, middle_count) in enumerate(counts_of(pieces)):
        number = jnp.where(code == near_count * (pieces + 1) + middle_count, i, number)
    front = jnp.where(count_near > 1, 1, 0)
    seen_near, seen_middle, seen_far = jnp.int32(0), count_near, count_near + count_middle
    for n in range(pieces):
        far = 1 - near[n] - middle[n]
        rank = near[n] * seen_near + middle[n] * seen_middle + far * seen_far
        seen_near, seen_middle, seen_far = seen_near + near[n], seen_middle + middle[n], seen_far + far
        line = jnp.where(number < RARE, pieces - 1 - rank, 2 * (rank % (pieces // 2)) + (rank // (pieces // 2) ^ front))
        plan_ref[line] = jnp.int32(n)
        plan_ref[pieces + n] = line
    plan_ref[2 * pieces] = number


def counts_of(pieces):
    counts = [(near, middle) for near in range(pieces + 1) for middle in range(pieces + 1 - near)]
    return sorted(counts, key=lambda c: (math.comb(pieces, c[0]) * math.comb(pieces - c[0], c[1]), c))


def over_elem(number, values, after, *args):
    pieces, groups = lax.axis_size("energy"), lax.axis_size("elem")

    def branch(number, near, middle):
        ranked = [1] * near + [2] * middle + [3] * (pieces - near - middle)
        rank = [pieces - 1 - n if number < RARE else n // 2 + pieces // 2 * (n % 2 ^ int(near > 1)) for n in range(pieces)]
        by_line = [ranked[rank[n]] for n in range(pieces)]
        pairs = [(n * groups + i, n * groups + (i ^ by_line[n])) for n in range(pieces) for i in range(groups)]
        return lambda sent, *args: after(lax.ppermute(sent, ("energy", "elem"), pairs), *args)

    return lax.switch(number, [branch(i, *counts) for i, counts in enumerate(counts_of(pieces))], values, *args)


def split_kernel(lists_ref, slots_ref, lesser_ref, greater_ref, *refs):
    (beside_ref, keep_ref, give_ref, number_ref, lines_ref, rows_ref, spots_ref) = refs[:7]
    lesser, greater, lists, slots, packed, scalars, plan_ref, sems = refs[7:]
    chip, core = place()
    pairs = [(lists_ref, scalars), (lists_ref, lists), (slots_ref, slots)]
    tile = keep_ref.shape[-1]
    for first in range(0, lesser.shape[-1], tile):
        cols = pl.ds(first, tile)
        pairs += [(source.at[:, :, cols], target.at[:, :, cols]) for source, target in ((lesser_ref, lesser), (greater_ref, greater))]
    copies = [pltpu.make_async_copy(source, target, sems.at[i]) for i, (source, target) in enumerate(pairs)]
    for copy in copies:
        copy.start()
    for copy in copies[:3]:
        copy.wait()
    distances(scalars, plan_ref)
    pieces = packed.shape[0]
    number_ref[0] = plan_ref[2 * pieces]
    lines_ref[...] = jnp.full(lines_ref.shape, sum(plan_ref[pieces + n] * 8**n for n in range(pieces)), jnp.int32)
    piece = plan_ref[2 * chip + core]
    rows_ref[...] = lists[piece]
    spots_ref[0:1, :] = slots[pl.ds(piece // 2, 1), :]
    spots_ref[1:2, :] = jnp.full((1, spots_ref.shape[1]), piece % 2, jnp.int32)
    for copy in copies[3:]:
        copy.wait()
    width = packed.shape[-1] // 2
    for n in range(pieces):
        cols = slice(n * width, (n + 1) * width)
        packed[n] = jnp.concatenate([lesser[:, :, cols], greater[:, :, cols]], axis=-1)
    for which in range(2):
        beside_ref[which] = packed[plan_ref[2 * (chip ^ 2) + which]]
    for i, j in enumerate((0, 1, 3)):
        keep_ref[i] = packed[plan_ref[2 * (chip ^ j) + core]]
        give_ref[i] = packed[plan_ref[2 * (chip ^ j) + 1 - core]]


def swap(values, axis, bit):
    return lax.ppermute(values, axis, [(i, i ^ bit) for i in range(lax.axis_size(axis))])


def collect_kernel(keep_ref, got_ref, diagonal_ref, across_ref, out_ref):
    out_ref[0], out_ref[1] = keep_ref[0], got_ref[0]
    for which in range(2):
        out_ref[2 + which] = across_ref[which]
        out_ref[4 + which] = diagonal_ref[which]


def over_energy(first, keep, give):
    beside = swap(first, "energy", 4)
    got = swap(give, "energy", 1)
    diagonal = swap(jnp.stack([keep[2], got[2]]), "energy", 6)
    across = swap(jnp.stack([keep[1], got[1]]), "energy", 2)
    early = jax.ShapeDtypeStruct((6, *keep.shape[1:]), BF16)
    early = call(collect_kernel, early, COLLECT_FLOPS, keep, got, diagonal, across)
    return early, beside, swap(beside, "energy", 1)


def blocks_of(refs, core):
    early_ref, beside_ref, beside_other_ref = refs
    early = [(lambda i=i: early_ref[i], lambda i=i: early_ref[i + 1]) for i in (0, 2, 4)]
    return [early[0], early[1], (lambda: beside_ref[core], lambda: beside_other_ref[core]), early[2]]


def lane_row(lanes):
    return lax.broadcasted_iota(jnp.int32, (1, lanes), 1)


def energies_of(device, energies):
    return pl.ds(pl.multiple_of(device * energies, energies), energies)


def repeat(values, index_row):
    return dot(values.astype(F32).astype(BF16), one_hot(index_row, values.shape[-1])).astype(jnp.int32)


def index_kernel(rows_ref, spots_ref, picks_ref):
    group = lax.axis_index("elem")
    lanes = picks_ref.shape[-1]
    width, cap = lanes // 2, lanes // 4
    lane = lane_row(lanes)
    lists = repeat(rows_ref[...], lane % cap)
    ids = lax.broadcasted_iota(jnp.int32, lists.shape, 0)
    greater = jnp.where(lane // cap % 2 == 1, width, 0)
    near_rows = jnp.sum(jnp.where(ids == group, lists, 0), axis=0, keepdims=True) + greater
    far_rows = jnp.sum(jnp.where(ids == group, 0, lists), axis=0, keepdims=True) + greater
    slots = spots_ref[0:1, :]
    twice = [repeat(slots, half * width + lane % width) for half in range(2)]
    slots = jnp.where(spots_ref[1:2, :] == 0, *twice)
    source = slots // cap
    spot = slots - source * cap + jnp.where(lane < width, cap, 0)
    near = one_hot(jnp.where(lane < 2 * cap, near_rows, -1), lanes)
    picks_ref[0] = dot(near, one_hot(jnp.where(source == group, spot, -1), lanes)).astype(BF16)
    for part in range(2):
        picks_ref[1 + part] = one_hot(jnp.where(source == group, -1, spot + 2 * cap * part), lanes)
        picks_ref[3 + part] = one_hot(jnp.where(lane // (2 * cap) == part, far_rows, -1), lanes)


def gather_kernel(picks_ref, *refs):
    in_refs, (signals_ref, sent_ref) = refs[:3], refs[3:]
    chip, core = place()
    energies, lanes = in_refs[0].shape[2:]
    for j, pair in enumerate(blocks_of(in_refs, core)):
        for which, block in enumerate(pair):
            values = block()
            rows = energies_of(2 * (chip ^ j) + (core if which == 0 else 1 - core), energies)
            for part in range(2):
                signals_ref[rows, part * lanes : (part + 1) * lanes] = values[part]
    sent_ref[...] = (dot(signals_ref[:, :lanes], picks_ref[3]) + dot(signals_ref[:, lanes:], picks_ref[4])).astype(BF16)


def own_kernel(signals_ref, picks_ref, table_ref, sums_ref, partner_ref, held_ref, sems):
    lanes = picks_ref.shape[-1]
    steps = sems.shape[0] // 4
    height = table_ref.shape[1] // steps
    copies = []
    for i in range(4 * steps):
        rows = pl.ds(i % steps * height, height)
        copies.append(pltpu.make_async_copy(table_ref.at[i // steps, rows], held_ref.at[i // steps, rows], sems.at[i]))
    for copy in copies:
        copy.start()
    for part in range(2):
        cols = slice(part * lanes, (part + 1) * lanes)
        partner_ref[:, cols] = dot(signals_ref[:, cols], picks_ref[0]).astype(BF16)
    for copy in copies:
        copy.wait()
    sums_ref[...] = forward_sums(held_ref, signals_ref[...])


def pick_kernel(near_ref, far_ref, picks_ref, partner_ref):
    lanes = picks_ref.shape[-1]
    far = far_ref[...]
    for part in range(2):
        cols = slice(part * lanes, (part + 1) * lanes)
        partner_ref[:, cols] = (near_ref[:, cols].astype(F32) + dot(far, picks_ref[1 + part])).astype(BF16)


def exchange_kernel(sums_ref, partner_ref, table_ref, *refs):
    (beside_ref, keep_ref, give_ref), (held,) = refs[:3], refs[3:]
    chip, core = place()
    energies, lanes = keep_ref.shape[2:]
    held[...] = correlate(sums_ref[...], forward_sums(table_ref, partner_ref[...]), table_ref)

    def block(j, core):
        rows = energies_of(2 * (chip ^ j) + core, energies)
        return [held[rows, part * lanes : (part + 1) * lanes] for part in range(2)]

    for which in range(2):
        beside_ref[which, 0], beside_ref[which, 1] = block(2, which)
    for i, j in enumerate((0, 1, 3)):
        keep_ref[i, 0], keep_ref[i, 1] = block(j, core)
        give_ref[i, 0], give_ref[i, 1] = block(j, 1 - core)


def join_kernel(lines_ref, *refs):
    in_refs, (lesser_ref, greater_ref, held) = refs[:3], refs[3:]
    chip, core = place()
    width = held.shape[-1] // 2
    for j, (mine, other) in enumerate(blocks_of(in_refs, core)):
        held[2 * (chip ^ j) + core] = mine()
        held[2 * (chip ^ j) + 1 - core] = other()
    lines = jnp.max(lines_ref[...])
    for n in range(0, held.shape[0], 2):
        even, odd = held[lines // 8**n % 8], held[lines // 8 ** (n + 1) % 8]
        cols = slice(n * width, (n + 2) * width)
        lesser_ref[:, :, cols] = jnp.concatenate([even[..., :width], odd[..., :width]], axis=-1)
        greater_ref[:, :, cols] = jnp.concatenate([even[..., width:], odd[..., width:]], axis=-1)


def four_chips(g_lesser, g_greater, send_rows, partner_slot):
    _, energies, group_rows = g_lesser.shape
    cap = send_rows.shape[-1]
    lanes = 4 * cap
    length = 8 * energies
    pair = jax.ShapeDtypeStruct((2, 2, energies, lanes), BF16)
    three = jax.ShapeDtypeStruct((3, 2, energies, lanes), BF16)
    leaving = [pair, three, three]
    column = jax.ShapeDtypeStruct((length, lanes), BF16)
    whole = jax.ShapeDtypeStruct((length, 2 * lanes), BF16)
    slots = partner_slot.reshape(4, lanes)
    table = jnp.asarray(fourier_tables(length))

    scratch = [
        pltpu.VMEM(g_lesser.shape, BF16),
        pltpu.VMEM(g_lesser.shape, BF16),
        pltpu.VMEM(send_rows.shape[1:], jnp.int32),
        pltpu.VMEM(slots.shape, jnp.int32),
        pltpu.VMEM((8, 2, energies, lanes), BF16),
        pltpu.SMEM(send_rows.shape[1:], jnp.int32),
        pltpu.SMEM((17,), jnp.int32),
        pltpu.SemaphoreType.DMA((11,)),
    ]
    more = [
        jax.ShapeDtypeStruct((1,), jnp.int32),
        jax.ShapeDtypeStruct((8, lanes), jnp.int32),
        jax.ShapeDtypeStruct((4, cap), jnp.int32),
        jax.ShapeDtypeStruct((2, lanes), jnp.int32),
    ]
    beside, keep, give, number, lines, rows, spots = call(
        split_kernel,
        leaving + more,
        2**24,
        send_rows[0],
        slots,
        g_lesser,
        g_greater,
        scratch=scratch,
        in_hbm=(0, 1, 2, 3),
        out_smem=(3,),
    )
    picks = call(index_kernel, jax.ShapeDtypeStruct((5, lanes, lanes), BF16), 2**24, rows, spots)
    beside, picks = lax.optimization_barrier((beside, picks))

    signals, sent = call(gather_kernel, [whole, column], 2**26, picks, *over_energy(beside, keep, give))

    def after(far, signals, picks, table):
        shapes = [jax.ShapeDtypeStruct(whole.shape, F32), whole, jax.ShapeDtypeStruct(table.shape, BF16)]
        sems = [pltpu.SemaphoreType.DMA((16,))]
        sums, near, held = call(own_kernel, shapes, 2**29, signals, picks, table, scratch=sems, in_hbm=(2,))
        return sums, call(pick_kernel, whole, 2**26, near, far, picks), held

    sums, partner, held = over_elem(number[0], sent, after, signals, picks, table)
    results = call(exchange_kernel, leaving, 2**30, sums, partner, held, scratch=[pltpu.VMEM(whole.shape, BF16)])
    out = jax.ShapeDtypeStruct((2, energies, group_rows), BF16)
    scratch = [pltpu.VMEM((8, 2, energies, lanes), BF16)]
    return tuple(call(join_kernel, [out, out], 0, lines, *over_energy(*results), scratch=scratch))


def any_mesh(g_lesser, g_greater, send_rows, partner_slot):
    piece = lax.axis_index("energy")
    pieces = lax.axis_size("energy")
    _, energies, group_rows = g_lesser.shape
    groups, cap = send_rows.shape[2:]
    width = group_rows // pieces
    lanes = 2 * width
    length = pieces * energies
    packed_shape = jax.ShapeDtypeStruct((pieces, 2, energies, lanes), BF16)
    packed = call(pack_kernel, packed_shape, 0, g_lesser, g_greater)
    own = lax.all_to_all(packed, "energy", split_axis=0, concat_axis=0, tiled=True)
    rows = lax.dynamic_index_in_dim(send_rows[0], piece, 0, keepdims=False).reshape(-1)
    slots = lax.dynamic_slice_in_dim(partner_slot, piece * width, width, 0)
    pick = (jnp.arange(width, dtype=jnp.int32)[:, None] == rows[None, :]).astype(BF16)
    split = own.reshape(pieces, 2, energies, 2, width)
    outgoing = jnp.einsum("pceds,sm->mpced", split, pick, preferred_element_type=F32).astype(BF16)
    incoming = lax.all_to_all(outgoing, "elem", split_axis=0, concat_axis=0, tiled=True)
    table_width = groups * cap
    far = jnp.transpose(incoming, (1, 3, 2, 4, 0)).reshape(length, 4 * table_width)
    index = jnp.concatenate([slots + table_width, slots])
    index = jnp.stack([index, index + 2 * table_width])
    result = call(
        correlate_kernel,
        packed_shape,
        2 * length * length * lanes * 14,
        index,
        own,
        far,
        jnp.asarray(fourier_tables(length)),
    )
    back = lax.all_to_all(result, "energy", split_axis=0, concat_axis=0, tiled=True)
    out = jax.ShapeDtypeStruct((2, energies, group_rows), BF16)
    return tuple(call(unpack_kernel, [out, out], 0, back))


def shards(g_lesser, g_greater, send_rows, partner_slot):
    _, pieces, groups, cap = send_rows.shape
    fits = pieces == 8 and groups == 4 and cap == 32 and partner_slot.shape[0] == 512
    path = four_chips if fits else any_mesh
    return path(g_lesser, g_greater, send_rows, partner_slot)


def solution(mesh):
    in_specs = (
        P(None, "energy", "elem"),
        P(None, "energy", "elem"),
        P("elem", None, None, None),
        P("elem"),
    )
    out_specs = (P(None, "energy", "elem"), P(None, "energy", "elem"))
    return jax.shard_map(shards, mesh=mesh, in_specs=in_specs, out_specs=out_specs, check_vma=False)
```
